256 devices in a mesh: group: 8 (over z), blk: 32 (over x, y, core).
Axes of the slice: x: 4, y: 4, z: 8, core: 2. Of those that a mesh axis runs over, the one named last changes fastest.
Arguments:
- image_a: float32 [3, 2048, 8192], P(None, 'group', 'blk'), may hold values from -6 to 6
- image_b: float32 [3, 2048, 8192], P(None, 'group', 'blk'), may hold values from -6 to 6
- initial: float32 [3, 2048, 8192], P(None, 'group', 'blk'), may hold values from -6 to 6
- coverage: int32 [8, 32], P('group', 'blk'), may hold values 0 or 1
- seam_label: int32 [8, 32], P('group', 'blk'), may hold values from 0 to 1
Outputs:
- blended: float32 [3, 2048, 8192], P(None, 'group', 'blk')
The draws below stay inside these ranges and needn't reach their ends.
All inputs are finite; a program needn't handle non-finite values. No bound on the sum of `coverage` on one device may be relied on, other than what follows from the above.
Results may differ from the reference program's by a relative error of at most 0.00003.
Values sent between devices are 32-bit elements; how exact they have to be, the bound alone decides.
A program may use at most 128 MiB of HBM per device.

```python
import jax
import jax.numpy as jnp

CHAN = 3
BS = 256
LEVELS = 4
NU = 2
COARSE = 4
NY = 2048
NX = 8192


def place_ends(result, rng, least, high):
    longest = result.shape.index(max(result.shape))
    spots = []
    for shift in (0, 1):
        where = [jax.random.randint(jax.random.fold_in(rng, axis), (), 0, length) for axis, length in enumerate(result.shape)]
        where[longest] = (where[longest] + shift) % result.shape[longest]
        spots.append(tuple(where))
    return result.at[spots[0]].set(least).at[spots[1]].set(high)


def shard_levels(key, dims, cuts, smallest, largest):
    loudness = 1.0
    for dim, shards_of in cuts:
        draws = jax.random.uniform(jax.random.fold_in(jax.random.fold_in(key, 6), dim), (shards_of,), jnp.float32, smallest / len(cuts), largest / len(cuts))
        loudness = loudness * jnp.repeat(jnp.exp(draws), dims[dim] // shards_of).reshape((-1,) + (1,) * (len(dims) - 1 - dim))
    return loudness


def bell_draw(own_key, dims, spread, bound, split=(), held_as=jnp.bfloat16):
    level = shard_levels(own_key, dims, split, -0.22, 0.18) if split else 1.0
    array = jax.random.normal(own_key, dims, jnp.float32) * spread * level
    return jnp.minimum(jnp.maximum(array, -bound), bound).astype(held_as)


def setup_inputs(seed: int = 0) -> dict:
    streams_of = jax.random.split(jax.random.key(seed), 6)
    return {
        "image_a": bell_draw(streams_of[0], (CHAN, NY, NX), 1.0, 6.0, ((1, 8), (2, 32)), jnp.float32),
        "image_b": bell_draw(streams_of[1], (CHAN, NY, NX), 1.0, 6.0, ((1, 8), (2, 32)), jnp.float32),
        "initial": bell_draw(streams_of[2], (CHAN, NY, NX), 1.0, 6.0, ((1, 8), (2, 32)), jnp.float32),
        "coverage": place_ends((jax.random.randint(streams_of[3], (NY // BS, NX // BS), 0, 4) < 3).astype(jnp.int32), jax.random.fold_in(streams_of[3], 1), 0, 1),
        "seam_label": place_ends(jax.random.randint(streams_of[4], (NY // BS, NX // BS), 0, 2), jax.random.fold_in(streams_of[4], 1), 0, 1).astype(jnp.int32),
    }


RELAX = 0.8


def beside_sum(padded):
    return padded[:, :-2, 1:-1] + padded[:, 2:, 1:-1] + padded[:, 1:-1, :-2] + padded[:, 1:-1, 2:]


def zero_rim(field):
    return jnp.pad(field, ((0, 0), (1, 1), (1, 1)))


def cell_map(table, span):
    return jnp.repeat(jnp.repeat(table, span, 0), span, 1)


def smooth(approx, source, active, depth_index, sweeps):
    factor = 0.25 ** depth_index
    for sweep in range(sweeps):
        approx = approx + RELAX * active * (source - factor * (4.0 * approx - beside_sum(zero_rim(approx)))) / (4.0 * factor)
    return approx


def shrink(field):
    chans, rows, cols = field.shape
    return field.reshape(chans, rows // 2, 2, cols // 2, 2).mean(axis=(2, 4))


def expand(field):
    return jnp.repeat(jnp.repeat(field, 2, 1), 2, 2)


def vcycle(source, depth_index, actives):
    active = actives[depth_index]
    zeros = jnp.zeros(source.shape, jnp.float32)
    if depth_index == LEVELS - 1:
        return smooth(zeros, source, active, depth_index, COARSE)
    approx = smooth(zeros, source, active, depth_index, NU)
    factor = 0.25 ** depth_index
    leftover = active * (source - factor * (4.0 * approx - beside_sum(zero_rim(approx))))
    coarse_fix = vcycle(shrink(leftover), depth_index + 1, actives)
    approx = approx + active * expand(coarse_fix)
    return smooth(approx, source, active, depth_index, NU)


def reference(image_a, image_b, initial, coverage, seam_label):
    actives = [cell_map(coverage, BS >> depth_index).astype(jnp.float32)[None] for depth_index in range(LEVELS)]
    laplace_a = 4.0 * image_a - beside_sum(zero_rim(image_a))
    laplace_b = 4.0 * image_b - beside_sum(zero_rim(image_b))
    laplace_x = 4.0 * initial - beside_sum(zero_rim(initial))
    labels = cell_map(seam_label, BS)[None]
    guide = jnp.where(labels == 1, laplace_b, laplace_a)
    source = actives[0] * (guide - laplace_x)
    return initial + vcycle(source, 0, actives)
```

```python
import functools

import jax
import jax.numpy as jnp
from jax import lax
from jax.experimental import pallas as pl
from jax.experimental.pallas import tpu as pltpu
from jax.sharding import PartitionSpec as P

MESH = pl.DeviceIdType.MESH
F32 = jnp.float32
CHAN = 3
BS = 256
LANES = 128
HALO = 16
ROWS0 = BS + 2 * HALO + 16
ROWS1 = BS // 2 + HALO + 16
ROWS2 = BS // 4 + 2 * HALO + 16
ROWS3 = BS // 8 + HALO + 16
OWN0 = 8 + HALO
OWN1 = 16
OWN2 = 8 + HALO
OWN3 = 16
NEIGHBOURS = ((-1, 1), (-1, -1), (1, 1), (1, -1), (0, 1), (0, -1), (-1, 0), (1, 0))


def tile(base):
    return pl.ds(pl.multiple_of(base, 8), 8)


def beside(ref, slabs, base, lane):
    centre = [ref[s, tile(base), :] for s in slabs]
    column = [ref[s, pl.ds(base - 1, 8), :] + ref[s, pl.ds(base + 1, 8), :] for s in slabs]
    right = [pltpu.roll(c, LANES - 1, 1) for c in centre]
    left = [pltpu.roll(c, 1, 1) for c in centre]
    n = len(slabs)
    if n > 1:
        right = [jnp.where(lane == LANES - 1, right[(i + 1) % n], right[i]) for i in range(n)]
        left = [jnp.where(lane == 0, left[(i - 1) % n], left[i]) for i in range(n)]
    return centre, [column[i] + (left[i] + right[i]) for i in range(n)]


def take(x, index):
    return jnp.take_along_axis(x, index, axis=1)


def kernel(groups, blks, a_hbm, b_hbm, x_hbm, cov, lab, out,
           a_in, b_in, x_in, d, dh, pe, pw, hw, he, mask, labels,
           s0, v0, w0, s1, v1, w1, s2, pe2, pw2, hw2, he2, s2x, v2, w2, s3, v3, w3,
           in_sem, send1, recv1, send2, recv2):
    g, k = lax.axis_index("group"), lax.axis_index("blk")
    lane = lax.broadcasted_iota(jnp.int32, (8, LANES), 1)
    zeros = jnp.zeros((8, LANES), F32)

    loads = [
        pltpu.make_async_copy(src, dst, in_sem.at[i])
        for i, (src, dst) in enumerate(((a_hbm, a_in), (b_hbm, b_in), (x_hbm, x_in)))
    ]
    for copy in loads:
        copy.start()

    def there(dg, dk):
        ok = None
        for at, step, size in ((g, dg, groups), (k, dk, blks)):
            if step:
                good = at < size - 1 if step > 0 else at > 0
                ok = good if ok is None else jnp.logical_and(ok, good)
        return ok

    for slab in range(13):
        for base in (8, 16, BS + OWN0, BS + OWN0 + 8):
            d[slab, base:base + 8, :] = zeros
    for ref in (hw, he):
        @pl.loop(0, ROWS0 // 8)
        def _(i):
            ref[tile(8 * i), :] = zeros
    for ref in (hw2, he2):
        for base in range(0, ROWS2, 8):
            ref[base:base + 8, :] = zeros
    for c in range(CHAN):
        for base in (8, 16, BS // 4 + OWN2, BS // 4 + OWN2 + 8):
            s2[c, base:base + 8, :] = zeros
    for ref, rows in ((s0, ROWS0), (v0, ROWS0), (w0, ROWS0), (s1, ROWS1), (v1, ROWS1), (w1, ROWS1),
                      (s2x, ROWS2), (v2, ROWS2), (w2, ROWS2), (s3, ROWS3), (v3, ROWS3), (w3, ROWS3),
                      (d, ROWS0), (dh, ROWS0)):
        for slab in range(ref.shape[0]):
            ref[slab, 0:8, :] = zeros
            ref[slab, rows - 8:rows, :] = zeros

    barrier = pltpu.get_barrier_semaphore()
    count = jnp.int32(0)
    for dg, dk in NEIGHBOURS:
        ok = there(dg, dk)
        count = count + ok.astype(jnp.int32)

        @pl.when(ok)
        def _():
            pl.semaphore_signal(barrier, inc=1, device_id=(g + dg, k + dk), device_id_type=MESH)

    my_cov = jnp.full((8, LANES), cov[0, 0].astype(F32), F32)
    my_lab = jnp.full((8, LANES), lab[0, 0].astype(F32), F32)
    for base in (OWN0, BS + OWN0 - HALO):
        d[12, base:base + 8, :] = my_lab
        d[12, base + 8:base + 16, :] = my_cov
    meta = jnp.where(lane < 112, my_lab, my_cov)

    for copy in loads:
        copy.wait()

    @pl.loop(0, BS // 8)
    def _(i):
        rows, to = tile(8 * i), tile(OWN0 + 8 * i)
        right, left = meta, meta
        for c in range(CHAN):
            for t in range(2):
                cols = slice(LANES * t, LANES * (t + 1))
                x = x_in[c, rows, cols]
                for f, ref in enumerate((a_in, b_in)):
                    field = f * CHAN + c
                    diff = ref[c, rows, cols] - x
                    d[2 * field + t, to, :] = diff
                    here = jnp.logical_and(lane >= 16 * field, lane < 16 * field + 16)
                    if t == 0:
                        left = jnp.where(here, pltpu.roll(diff, 16 * field, 1), left)
                    else:
                        right = jnp.where(here, pltpu.roll(diff, (16 * field + 16) % LANES, 1), right)
        pe[rows, :] = right
        pw[rows, :] = left

    pl.semaphore_wait(barrier, count)

    def exchange(main, east, west, from_w, from_e, own, size, send, recv):
        n, top, low = HALO, own - HALO, own + size
        src_dst = {
            (-1, 1): (east.at[0:n], from_w.at[low:low + n]),
            (-1, -1): (west.at[0:n], from_e.at[low:low + n]),
            (1, 1): (east.at[size - n:size], from_w.at[top:top + n]),
            (1, -1): (west.at[size - n:size], from_e.at[top:top + n]),
            (0, 1): (east, from_w.at[own:own + size]),
            (0, -1): (west, from_e.at[own:own + size]),
            (-1, 0): (main.at[:, own:own + n, :], main.at[:, low:low + n, :]),
            (1, 0): (main.at[:, low - n:low, :], main.at[:, top:top + n, :]),
        }

        def copy_to(i, dg, dk):
            src, dst = src_dst[dg, dk]
            return pltpu.make_async_remote_copy(
                src_ref=src, dst_ref=dst, send_sem=send.at[i], recv_sem=recv.at[i],
                device_id=(g + dg, k + dk), device_id_type=MESH)

        for i, (dg, dk) in enumerate(NEIGHBOURS):
            @pl.when(there(dg, dk))
            def _():
                copy_to(i, dg, dk).start()

        def finish():
            for i, (dg, dk) in enumerate(NEIGHBOURS):
                @pl.when(there(-dg, -dk))
                def _():
                    copy_to(i, dg, dk).wait_recv()
            for i, (dg, dk) in enumerate(NEIGHBOURS):
                @pl.when(there(dg, dk))
                def _():
                    copy_to(i, dg, dk).wait_send()

        return finish

    exchange(d, pe, pw, hw, he, OWN0, BS, send1, recv1)()

    for z, base in enumerate((8, OWN0, BS + OWN0)):
        west, east = hw[base:base + 8, :], he[base:base + 8, :]
        at = lambda where: jnp.full((8, LANES), where, jnp.int32)
        lab_w, cov_w = take(west, at(96)), take(west, at(112))
        lab_e, cov_e = take(east, at(96)), take(east, at(112))
        lab_z, cov_z = (my_lab, my_cov) if z == 1 else (d[12, base:base + 8, :], d[12, base + 8:base + 16, :])
        mask[z, 0] = cov_z
        mask[z, 1] = jnp.where(lane < 64, cov_e, cov_w)
        mask[z, 2] = jnp.where(lane < 64, cov_z, jnp.where(lane < 96, cov_e, cov_w))
        mask[z, 3] = jnp.where(lane < 32, cov_z, jnp.where(lane < 80, cov_e, cov_w))
        labels[z, 0] = lab_z
        labels[z, 1] = jnp.where(lane < 64, lab_e, lab_w)

    def zone(i, before, own):
        return jnp.where(i < before, 0, jnp.where(i < before + own, 1, 2))

    @pl.loop(1, ROWS0 // 8 - 1)
    def _(i):
        west, east = hw[tile(8 * i), :], he[tile(8 * i), :]
        for f in range(2 * CHAN):
            side = jnp.where(lane < 16, pltpu.roll(east, (LANES - 16 * f) % LANES, 1), 0.0)
            dh[f, tile(8 * i), :] = jnp.where(lane >= 112, pltpu.roll(west, 112 - 16 * f, 1), side)

    def slabs0(c):
        return [3 * c, 3 * c + 1, 3 * c + 2]

    tiles0 = ROWS0 // 8 - 2

    def beside_d(field, base):
        refs = [d.at[2 * field], d.at[2 * field + 1], dh.at[field]]
        centre = [r[tile(base), :] for r in refs]
        column = [r[pl.ds(base - 1, 8), :] + r[pl.ds(base + 1, 8), :] for r in refs]
        right = [pltpu.roll(x, LANES - 1, 1) for x in centre]
        left = [pltpu.roll(x, 1, 1) for x in centre]
        right = [jnp.where(lane == LANES - 1, right[(i + 1) % 3], right[i]) for i in range(3)]
        left = [jnp.where(lane == 0, left[(i - 1) % 3], left[i]) for i in range(3)]
        return [4.0 * centre[i] - (column[i] + (left[i] + right[i])) for i in range(3)]

    @pl.loop(0, tiles0)
    def _(i):
        z = zone(i, 2, 32)
        base = 8 + 8 * i
        for c in range(CHAN):
            la, lb = beside_d(c, base), beside_d(CHAN + c, base)
            for t in range(3):
                kind = t // 2
                s0[3 * c + t, tile(base), :] = mask[z, kind] * jnp.where(labels[z, kind] == 1.0, lb[t], la[t])

    def down(s, v, w, tiles, zones, kinds, slabs_of):
        @pl.loop(0, tiles)
        def _(i):
            z, base = zone(i, *zones), 8 + 8 * i
            act = [mask[z, kind] * 0.04 for kind in sorted(set(kinds))]
            first = min(kinds)
            for c in range(CHAN):
                slabs = slabs_of(c)
                centre, around = beside(s, slabs, base, lane)
                for j, slab in enumerate(slabs):
                    v[slab, tile(base), :] = act[kinds[j] - first] * (6.0 * centre[j] + around[j])

        @pl.loop(0, tiles)
        def _(i):
            z, base = zone(i, *zones), 8 + 8 * i
            for c in range(CHAN):
                slabs = slabs_of(c)
                centre, around = beside(v, slabs, base, lane)
                for j, slab in enumerate(slabs):
                    w[slab, tile(base), :] = mask[z, kinds[j]] * (
                        s[slab, tile(base), :] + (around[j] - 4.0 * centre[j]))

    def sweep(s, v, w, start, tiles, zones, kinds, slabs_of):
        @pl.loop(start, start + tiles)
        def _(i):
            z, base = zone(i, *zones), 8 + 8 * i
            act = [mask[z, kind] * 0.2 for kind in sorted(set(kinds))]
            first = min(kinds)
            for c in range(CHAN):
                slabs = slabs_of(c)
                centre, around = beside(v, slabs, base, lane)
                for j, slab in enumerate(slabs):
                    w[slab, tile(base), :] = act[kinds[j] - first] * (
                        centre[j] + around[j] + s[slab, tile(base), :])

    def pair_rows(ref, slab, base):
        total = ref[slab, pl.ds(base, 8, stride=2), :] + ref[slab, pl.ds(base + 1, 8, stride=2), :]
        return total + pltpu.roll(total, LANES - 1, 1)

    twice = lax.rem(2 * lane, LANES)
    low, high = lane // 2, lane // 2 + 64

    down(s0, v0, w0, tiles0, (2, 32), (0, 0, 1), slabs0)

    tiles1 = ROWS1 // 8 - 2

    def slabs1(c):
        return [2 * c, 2 * c + 1]

    @pl.loop(0, tiles1)
    def _(i):
        fine, base = 8 + 16 * i, 8 + 8 * i
        for c in range(CHAN):
            x, y, h = (pair_rows(w0, 3 * c + t, fine) for t in range(3))
            s1[2 * c, tile(base), :] = jnp.where(lane < 64, take(x, twice), take(y, twice))
            s1[2 * c + 1, tile(base), :] = take(h, twice)

    down(s1, v1, w1, tiles1, (1, 16), (0, 1), slabs1)

    @pl.loop(0, BS // 32)
    def _(i):
        right, left = zeros, zeros
        for c in range(CHAN):
            x = take(pair_rows(w1, 2 * c, OWN1 + 16 * i), twice)
            s2[c, tile(OWN2 + 8 * i), :] = x
            here = jnp.logical_and(lane >= 16 * c, lane < 16 * c + 16)
            left = jnp.where(here, pltpu.roll(x, 16 * c, 1), left)
            right = jnp.where(here, pltpu.roll(x, (16 * c - 48) % LANES, 1), right)
        pe2[tile(8 * i), :] = right
        pw2[tile(8 * i), :] = left

    exchange(s2, pe2, pw2, hw2, he2, OWN2, BS // 4, send2, recv2)()

    tiles2 = ROWS2 // 8 - 2

    @pl.loop(0, tiles2)
    def _(i):
        rows = tile(8 + 8 * i)
        west, east = hw2[rows, :], he2[rows, :]
        for c in range(CHAN):
            side = jnp.where(lane < 80, pltpu.roll(east, (64 - 16 * c) % LANES, 1), 0.0)
            side = jnp.where(lane >= 112, pltpu.roll(west, 112 - 16 * c, 1), side)
            s2x[c, rows, :] = jnp.where(lane < 64, s2[c, rows, :], side)

    def slabs2(c):
        return [c]

    down(s2x, v2, w2, tiles2, (2, 8), (2,), slabs2)

    tiles3 = ROWS3 // 8 - 2

    @pl.loop(0, tiles3)
    def _(i):
        for c in range(CHAN):
            s3[c, tile(8 + 8 * i), :] = take(pair_rows(w2, c, 8 + 16 * i), twice)

    @pl.loop(0, tiles3)
    def _(i):
        z, base = zone(i, 1, 4), 8 + 8 * i
        for c in range(CHAN):
            (centre,), (around,) = beside(s3, [c], base, lane)
            v3[c, tile(base), :] = 0.04 * mask[z, 3] * (6.0 * centre + around)

    sweep(s3, v3, w3, 0, tiles3, (1, 4), (3,), slabs2)
    sweep(s3, w3, v3, 0, tiles3, (1, 4), (3,), slabs2)

    def add_up(v, slab, fine, act, value):
        for half in range(2):
            rows = pl.ds(fine + half, 8, stride=2)
            v[slab, rows, :] = v[slab, rows, :] + act * value

    @pl.loop(0, tiles3)
    def _(i):
        act = mask[zone(i, 1, 4), 2]
        for c in range(CHAN):
            value = v3[c, tile(8 + 8 * i), :]
            add_up(v2, c, 8 + 16 * i, act, take(value, jnp.where(lane < 96, low, high)))

    sweep(s2x, v2, w2, 0, tiles2, (2, 8), (2,), slabs2)
    sweep(s2x, w2, v2, 0, tiles2, (2, 8), (2,), slabs2)

    @pl.loop(0, ROWS1 // 16)
    def _(i):
        z = zone(i, 1, 8)
        for c in range(CHAN):
            value = v2[c, tile(OWN2 - 8 + 8 * i), :]
            add_up(v1, 2 * c, 16 * i, mask[z, 0], take(value, low))
            add_up(v1, 2 * c + 1, 16 * i, mask[z, 1], take(value, high))

    sweep(s1, v1, w1, 0, tiles1, (1, 16), (0, 1), slabs1)
    sweep(s1, w1, v1, 0, tiles1, (1, 16), (0, 1), slabs1)

    @pl.loop(0, tiles1)
    def _(i):
        z, fine = zone(i, 1, 16), 8 + 16 * i
        for c in range(CHAN):
            value, beyond = v1[2 * c, tile(8 + 8 * i), :], v1[2 * c + 1, tile(8 + 8 * i), :]
            add_up(v0, 3 * c, fine, mask[z, 0], take(value, low))
            add_up(v0, 3 * c + 1, fine, mask[z, 0], take(value, high))
            add_up(v0, 3 * c + 2, fine, mask[z, 1], take(beyond, jnp.where(lane < 64, low, high)))

    sweep(s0, v0, w0, 1, tiles0 - 2, (2, 32), (0, 0, 1), slabs0)

    act = mask[1, 0] * 0.2

    @pl.loop(0, BS // 8)
    def _(i):
        base = OWN0 + 8 * i
        for c in range(CHAN):
            centre, around = beside(w0, slabs0(c), base, lane)
            for t in range(2):
                cols = slice(LANES * t, LANES * (t + 1))
                out[c, tile(8 * i), cols] = x_in[c, tile(8 * i), cols] + act * (
                    centre[t] + around[t] + s0[3 * c + t, tile(base), :])


def shards(groups, blks, image_a, image_b, initial, coverage, seam_label):
    vmem = lambda *dims: pltpu.VMEM(dims, F32)
    image = vmem(CHAN, BS, BS)
    scratch = [image] * 3
    scratch += [vmem(13, ROWS0, LANES), vmem(6, ROWS0, LANES)]
    scratch += [vmem(BS, LANES)] * 2 + [vmem(ROWS0, LANES)] * 2
    scratch += [vmem(3, 4, 8, LANES), vmem(3, 2, 8, LANES)]
    scratch += [vmem(9, ROWS0, LANES)] * 3 + [vmem(6, ROWS1, LANES)] * 3
    scratch += [vmem(3, ROWS2, LANES)] + [vmem(BS // 4, LANES)] * 2 + [vmem(ROWS2, LANES)] * 2
    scratch += [vmem(3, ROWS2, LANES)] * 3 + [vmem(3, ROWS3, LANES)] * 3
    scratch += [pltpu.SemaphoreType.DMA((3,))] + [pltpu.SemaphoreType.DMA((8,))] * 4
    return pl.pallas_call(
        functools.partial(kernel, groups, blks),
        out_shape=jax.ShapeDtypeStruct(image_a.shape, F32),
        in_specs=[pl.BlockSpec(memory_space=pl.ANY)] * 3 + [pl.BlockSpec(memory_space=pltpu.SMEM)] * 2,
        out_specs=pl.BlockSpec(memory_space=pltpu.VMEM),
        scratch_shapes=scratch,
        compiler_params=pltpu.CompilerParams(
            collective_id=0, has_side_effects=True, vmem_limit_bytes=40 << 20),
    )(image_a, image_b, initial, coverage, seam_label)


def solution(mesh):
    placed = (P(None, "group", "blk"),) * 3 + (P("group", "blk"),) * 2
    return jax.shard_map(
        functools.partial(shards, mesh.shape["group"], mesh.shape["blk"]),
        mesh=mesh, in_specs=placed, out_specs=P(None, "group", "blk"), check_vma=False)
```

```python
import functools

import jax
import jax.numpy as jnp
from jax import lax
from jax.experimental import pallas as pl
from jax.experimental.pallas import tpu as pltpu
from jax.sharding import PartitionSpec as P

MESH = pl.DeviceIdType.MESH
F32 = jnp.float32
CHAN = 3
BS = 256
LANES = 128
HALO = 16
ROWS0 = BS + 2 * HALO + 16
ROWS1 = BS // 2 + HALO + 16
ROWS2 = BS // 4 + 2 * HALO + 16
ROWS3 = BS // 8 + HALO + 16
OWN0 = 8 + HALO
OWN1 = 16
OWN2 = 8 + HALO
OWN3 = 16
NEIGHBOURS = ((-1, 1), (-1, -1), (1, 1), (1, -1), (0, 1), (0, -1), (-1, 0), (1, 0))


def tile(base):
    return pl.ds(pl.multiple_of(base, 8), 8)


def beside(ref, slabs, base, lane):
    centre = [ref[s, tile(base), :] for s in slabs]
    column = [ref[s, pl.ds(base - 1, 8), :] + ref[s, pl.ds(base + 1, 8), :] for s in slabs]
    right = [pltpu.roll(c, LANES - 1, 1) for c in centre]
    left = [pltpu.roll(c, 1, 1) for c in centre]
    n = len(slabs)
    if n > 1:
        right = [jnp.where(lane == LANES - 1, right[(i + 1) % n], right[i]) for i in range(n)]
        left = [jnp.where(lane == 0, left[(i - 1) % n], left[i]) for i in range(n)]
    return centre, [column[i] + (left[i] + right[i]) for i in range(n)]


def take(x, index):
    return jnp.take_along_axis(x, index, axis=1)


def kernel(groups, blks, a_hbm, b_hbm, x_hbm, cov, lab, out,
           a_in, b_in, x_in, d, dh, pe, pw, hw, he, mask, labels,
           s0, v0, w0, s1, v1, w1, s2, pe2, pw2, hw2, he2, s2x, v2, w2, s3, v3, w3,
           in_sem, send1, recv1, send2, recv2):
    g, k = lax.axis_index("group"), lax.axis_index("blk")
    lane = lax.broadcasted_iota(jnp.int32, (8, LANES), 1)
    zeros = jnp.zeros((8, LANES), F32)

    loads = [
        pltpu.make_async_copy(src, dst, in_sem.at[i])
        for i, (src, dst) in enumerate(((a_hbm, a_in), (b_hbm, b_in), (x_hbm, x_in)))
    ]
    for copy in loads:
        copy.start()

    def there(dg, dk):
        ok = None
        for at, step, size in ((g, dg, groups), (k, dk, blks)):
            if step:
                good = at < size - 1 if step > 0 else at > 0
                ok = good if ok is None else jnp.logical_and(ok, good)
        return ok

    for slab in range(13):
        for base in (8, 16, BS + OWN0, BS + OWN0 + 8):
            d[slab, base:base + 8, :] = zeros
    for ref in (hw, he):
        @pl.loop(0, ROWS0 // 8, unroll=True)
        def _(i):
            ref[tile(8 * i), :] = zeros
    for ref in (hw2, he2):
        for base in range(0, ROWS2, 8):
            ref[base:base + 8, :] = zeros
    for c in range(CHAN):
        for base in (8, 16, BS // 4 + OWN2, BS // 4 + OWN2 + 8):
            s2[c, base:base + 8, :] = zeros
    for ref, rows in ((s0, ROWS0), (v0, ROWS0), (w0, ROWS0), (s1, ROWS1), (v1, ROWS1), (w1, ROWS1),
                      (s2x, ROWS2), (v2, ROWS2), (w2, ROWS2), (s3, ROWS3), (v3, ROWS3), (w3, ROWS3),
                      (d, ROWS0), (dh, ROWS0)):
        for slab in range(ref.shape[0]):
            ref[slab, 0:8, :] = zeros
            ref[slab, rows - 8:rows, :] = zeros

    barrier = pltpu.get_barrier_semaphore()
    count = jnp.int32(0)
    for dg, dk in NEIGHBOURS:
        ok = there(dg, dk)
        count = count + ok.astype(jnp.int32)

        @pl.when(ok)
        def _():
            pl.semaphore_signal(barrier, inc=1, device_id=(g + dg, k + dk), device_id_type=MESH)

    my_cov = jnp.full((8, LANES), cov[0, 0].astype(F32), F32)
    my_lab = jnp.full((8, LANES), lab[0, 0].astype(F32), F32)
    for base in (OWN0, BS + OWN0 - HALO):
        d[12, base:base + 8, :] = my_lab
        d[12, base + 8:base + 16, :] = my_cov
    meta = jnp.where(lane < 112, my_lab, my_cov)

    for copy in loads:
        copy.wait()

    @pl.loop(0, BS // 8, unroll=True)
    def _(i):
        rows, to = tile(8 * i), tile(OWN0 + 8 * i)
        right, left = meta, meta
        for c in range(CHAN):
            for t in range(2):
                cols = slice(LANES * t, LANES * (t + 1))
                x = x_in[c, rows, cols]
                for f, ref in enumerate((a_in, b_in)):
                    field = f * CHAN + c
                    diff = ref[c, rows, cols] - x
                    d[2 * field + t, to, :] = diff
                    here = jnp.logical_and(lane >= 16 * field, lane < 16 * field + 16)
                    if t == 0:
                        left = jnp.where(here, pltpu.roll(diff, 16 * field, 1), left)
                    else:
                        right = jnp.where(here, pltpu.roll(diff, (16 * field + 16) % LANES, 1), right)
        pe[rows, :] = right
        pw[rows, :] = left

    pl.semaphore_wait(barrier, count)

    def exchange(main, east, west, from_w, from_e, own, size, send, recv):
        n, top, low = HALO, own - HALO, own + size
        src_dst = {
            (-1, 1): (east.at[0:n], from_w.at[low:low + n]),
            (-1, -1): (west.at[0:n], from_e.at[low:low + n]),
            (1, 1): (east.at[size - n:size], from_w.at[top:top + n]),
            (1, -1): (west.at[size - n:size], from_e.at[top:top + n]),
            (0, 1): (east, from_w.at[own:own + size]),
            (0, -1): (west, from_e.at[own:own + size]),
            (-1, 0): (main.at[:, own:own + n, :], main.at[:, low:low + n, :]),
            (1, 0): (main.at[:, low - n:low, :], main.at[:, top:top + n, :]),
        }

        def copy_to(i, dg, dk):
            src, dst = src_dst[dg, dk]
            return pltpu.make_async_remote_copy(
                src_ref=src, dst_ref=dst, send_sem=send.at[i], recv_sem=recv.at[i],
                device_id=(g + dg, k + dk), device_id_type=MESH)

        for i, (dg, dk) in enumerate(NEIGHBOURS):
            @pl.when(there(dg, dk))
            def _():
                copy_to(i, dg, dk).start()

        def finish():
            for i, (dg, dk) in enumerate(NEIGHBOURS):
                @pl.when(there(-dg, -dk))
                def _():
                    copy_to(i, dg, dk).wait_recv()
            for i, (dg, dk) in enumerate(NEIGHBOURS):
                @pl.when(there(dg, dk))
                def _():
                    copy_to(i, dg, dk).wait_send()

        return finish

    exchange(d, pe, pw, hw, he, OWN0, BS, send1, recv1)()

    for z, base in enumerate((8, OWN0, BS + OWN0)):
        west, east = hw[base:base + 8, :], he[base:base + 8, :]
        at = lambda where: jnp.full((8, LANES), where, jnp.int32)
        lab_w, cov_w = take(west, at(96)), take(west, at(112))
        lab_e, cov_e = take(east, at(96)), take(east, at(112))
        lab_z, cov_z = (my_lab, my_cov) if z == 1 else (d[12, base:base + 8, :], d[12, base + 8:base + 16, :])
        mask[z, 0] = cov_z
        mask[z, 1] = jnp.where(lane < 64, cov_e, cov_w)
        mask[z, 2] = jnp.where(lane < 64, cov_z, jnp.where(lane < 96, cov_e, cov_w))
        mask[z, 3] = jnp.where(lane < 32, cov_z, jnp.where(lane < 80, cov_e, cov_w))
        labels[z, 0] = lab_z
        labels[z, 1] = jnp.where(lane < 64, lab_e, lab_w)

    def zone(i, before, own):
        return jnp.where(i < before, 0, jnp.where(i < before + own, 1, 2))

    @pl.loop(1, ROWS0 // 8 - 1, unroll=True)
    def _(i):
        west, east = hw[tile(8 * i), :], he[tile(8 * i), :]
        for f in range(2 * CHAN):
            side = jnp.where(lane < 16, pltpu.roll(east, (LANES - 16 * f) % LANES, 1), 0.0)
            dh[f, tile(8 * i), :] = jnp.where(lane >= 112, pltpu.roll(west, 112 - 16 * f, 1), side)

    def slabs0(c):
        return [3 * c, 3 * c + 1, 3 * c + 2]

    tiles0 = ROWS0 // 8 - 2

    def beside_d(field, base):
        refs = [d.at[2 * field], d.at[2 * field + 1], dh.at[field]]
        centre = [r[tile(base), :] for r in refs]
        column = [r[pl.ds(base - 1, 8), :] + r[pl.ds(base + 1, 8), :] for r in refs]
        right = [pltpu.roll(x, LANES - 1, 1) for x in centre]
        left = [pltpu.roll(x, 1, 1) for x in centre]
        right = [jnp.where(lane == LANES - 1, right[(i + 1) % 3], right[i]) for i in range(3)]
        left = [jnp.where(lane == 0, left[(i - 1) % 3], left[i]) for i in range(3)]
        return [4.0 * centre[i] - (column[i] + (left[i] + right[i])) for i in range(3)]

    @pl.loop(0, tiles0, unroll=True)
    def _(i):
        z = zone(i, 2, 32)
        base = 8 + 8 * i
        for c in range(CHAN):
            la, lb = beside_d(c, base), beside_d(CHAN + c, base)
            for t in range(3):
                kind = t // 2
                s0[3 * c + t, tile(base), :] = mask[z, kind] * jnp.where(labels[z, kind] == 1.0, lb[t], la[t])

    def down(s, v, w, tiles, zones, kinds, slabs_of):
        @pl.loop(0, tiles, unroll=True)
        def _(i):
            z, base = zone(i, *zones), 8 + 8 * i
            act = [mask[z, kind] * 0.04 for kind in sorted(set(kinds))]
            first = min(kinds)
            for c in range(CHAN):
                slabs = slabs_of(c)
                centre, around = beside(s, slabs, base, lane)
                for j, slab in enumerate(slabs):
                    v[slab, tile(base), :] = act[kinds[j] - first] * (6.0 * centre[j] + around[j])

        @pl.loop(0, tiles, unroll=True)
        def _(i):
            z, base = zone(i, *zones), 8 + 8 * i
            for c in range(CHAN):
                slabs = slabs_of(c)
                centre, around = beside(v, slabs, base, lane)
                for j, slab in enumerate(slabs):
                    w[slab, tile(base), :] = mask[z, kinds[j]] * (
                        s[slab, tile(base), :] + (around[j] - 4.0 * centre[j]))

    def sweep(s, v, w, start, tiles, zones, kinds, slabs_of):
        @pl.loop(start, start + tiles, unroll=True)
        def _(i):
            z, base = zone(i, *zones), 8 + 8 * i
            act = [mask[z, kind] * 0.2 for kind in sorted(set(kinds))]
            first = min(kinds)
            for c in range(CHAN):
                slabs = slabs_of(c)
                centre, around = beside(v, slabs, base, lane)
                for j, slab in enumerate(slabs):
                    w[slab, tile(base), :] = act[kinds[j] - first] * (
                        centre[j] + around[j] + s[slab, tile(base), :])

    def pair_rows(ref, slab, base):
        total = ref[slab, pl.ds(base, 8, stride=2), :] + ref[slab, pl.ds(base + 1, 8, stride=2), :]
        return total + pltpu.roll(total, LANES - 1, 1)

    twice = lax.rem(2 * lane, LANES)
    low, high = lane // 2, lane // 2 + 64

    down(s0, v0, w0, tiles0, (2, 32), (0, 0, 1), slabs0)

    tiles1 = ROWS1 // 8 - 2

    def slabs1(c):
        return [2 * c, 2 * c + 1]

    @pl.loop(0, tiles1, unroll=True)
    def _(i):
        fine, base = 8 + 16 * i, 8 + 8 * i
        for c in range(CHAN):
            x, y, h = (pair_rows(w0, 3 * c + t, fine) for t in range(3))
            s1[2 * c, tile(base), :] = jnp.where(lane < 64, take(x, twice), take(y, twice))
            s1[2 * c + 1, tile(base), :] = take(h, twice)

    down(s1, v1, w1, tiles1, (1, 16), (0, 1), slabs1)

    @pl.loop(0, BS // 32, unroll=True)
    def _(i):
        right, left = zeros, zeros
        for c in range(CHAN):
            x = take(pair_rows(w1, 2 * c, OWN1 + 16 * i), twice)
            s2[c, tile(OWN2 + 8 * i), :] = x
            here = jnp.logical_and(lane >= 16 * c, lane < 16 * c + 16)
            left = jnp.where(here, pltpu.roll(x, 16 * c, 1), left)
            right = jnp.where(here, pltpu.roll(x, (16 * c - 48) % LANES, 1), right)
        pe2[tile(8 * i), :] = right
        pw2[tile(8 * i), :] = left

    exchange(s2, pe2, pw2, hw2, he2, OWN2, BS // 4, send2, recv2)()

    tiles2 = ROWS2 // 8 - 2

    @pl.loop(0, tiles2, unroll=True)
    def _(i):
        rows = tile(8 + 8 * i)
        west, east = hw2[rows, :], he2[rows, :]
        for c in range(CHAN):
            side = jnp.where(lane < 80, pltpu.roll(east, (64 - 16 * c) % LANES, 1), 0.0)
            side = jnp.where(lane >= 112, pltpu.roll(west, 112 - 16 * c, 1), side)
            s2x[c, rows, :] = jnp.where(lane < 64, s2[c, rows, :], side)

    def slabs2(c):
        return [c]

    down(s2x, v2, w2, tiles2, (2, 8), (2,), slabs2)

    tiles3 = ROWS3 // 8 - 2

    @pl.loop(0, tiles3, unroll=True)
    def _(i):
        for c in range(CHAN):
            s3[c, tile(8 + 8 * i), :] = take(pair_rows(w2, c, 8 + 16 * i), twice)

    @pl.loop(0, tiles3, unroll=True)
    def _(i):
        z, base = zone(i, 1, 4), 8 + 8 * i
        for c in range(CHAN):
            (centre,), (around,) = beside(s3, [c], base, lane)
            v3[c, tile(base), :] = 0.04 * mask[z, 3] * (6.0 * centre + around)

    sweep(s3, v3, w3, 0, tiles3, (1, 4), (3,), slabs2)
    sweep(s3, w3, v3, 0, tiles3, (1, 4), (3,), slabs2)

    def add_up(v, slab, fine, act, value):
        for half in range(2):
            rows = pl.ds(fine + half, 8, stride=2)
            v[slab, rows, :] = v[slab, rows, :] + act * value

    @pl.loop(0, tiles3, unroll=True)
    def _(i):
        act = mask[zone(i, 1, 4), 2]
        for c in range(CHAN):
            value = v3[c, tile(8 + 8 * i), :]
            add_up(v2, c, 8 + 16 * i, act, take(value, jnp.where(lane < 96, low, high)))

    sweep(s2x, v2, w2, 0, tiles2, (2, 8), (2,), slabs2)
    sweep(s2x, w2, v2, 0, tiles2, (2, 8), (2,), slabs2)

    @pl.loop(0, ROWS1 // 16, unroll=True)
    def _(i):
        z = zone(i, 1, 8)
        for c in range(CHAN):
            value = v2[c, tile(OWN2 - 8 + 8 * i), :]
            add_up(v1, 2 * c, 16 * i, mask[z, 0], take(value, low))
            add_up(v1, 2 * c + 1, 16 * i, mask[z, 1], take(value, high))

    sweep(s1, v1, w1, 0, tiles1, (1, 16), (0, 1), slabs1)
    sweep(s1, w1, v1, 0, tiles1, (1, 16), (0, 1), slabs1)

    @pl.loop(0, tiles1, unroll=True)
    def _(i):
        z, fine = zone(i, 1, 16), 8 + 16 * i
        for c in range(CHAN):
            value, beyond = v1[2 * c, tile(8 + 8 * i), :], v1[2 * c + 1, tile(8 + 8 * i), :]
            add_up(v0, 3 * c, fine, mask[z, 0], take(value, low))
            add_up(v0, 3 * c + 1, fine, mask[z, 0], take(value, high))
            add_up(v0, 3 * c + 2, fine, mask[z, 1], take(beyond, jnp.where(lane < 64, low, high)))

    sweep(s0, v0, w0, 1, tiles0 - 2, (2, 32), (0, 0, 1), slabs0)

    act = mask[1, 0] * 0.2

    @pl.loop(0, BS // 8, unroll=True)
    def _(i):
        base = OWN0 + 8 * i
        for c in range(CHAN):
            centre, around = beside(w0, slabs0(c), base, lane)
            for t in range(2):
                cols = slice(LANES * t, LANES * (t + 1))
                out[c, tile(8 * i), cols] = x_in[c, tile(8 * i), cols] + act * (
                    centre[t] + around[t] + s0[3 * c + t, tile(base), :])


def shards(groups, blks, image_a, image_b, initial, coverage, seam_label):
    vmem = lambda *dims: pltpu.VMEM(dims, F32)
    image = vmem(CHAN, BS, BS)
    scratch = [image] * 3
    scratch += [vmem(13, ROWS0, LANES), vmem(6, ROWS0, LANES)]
    scratch += [vmem(BS, LANES)] * 2 + [vmem(ROWS0, LANES)] * 2
    scratch += [vmem(3, 4, 8, LANES), vmem(3, 2, 8, LANES)]
    scratch += [vmem(9, ROWS0, LANES)] * 3 + [vmem(6, ROWS1, LANES)] * 3
    scratch += [vmem(3, ROWS2, LANES)] + [vmem(BS // 4, LANES)] * 2 + [vmem(ROWS2, LANES)] * 2
    scratch += [vmem(3, ROWS2, LANES)] * 3 + [vmem(3, ROWS3, LANES)] * 3
    scratch += [pltpu.SemaphoreType.DMA((3,))] + [pltpu.SemaphoreType.DMA((8,))] * 4
    return pl.pallas_call(
        functools.partial(kernel, groups, blks),
        out_shape=jax.ShapeDtypeStruct(image_a.shape, F32),
        in_specs=[pl.BlockSpec(memory_space=pl.ANY)] * 3 + [pl.BlockSpec(memory_space=pltpu.SMEM)] * 2,
        out_specs=pl.BlockSpec(memory_space=pltpu.VMEM),
        scratch_shapes=scratch,
        compiler_params=pltpu.CompilerParams(
            collective_id=0, has_side_effects=True, vmem_limit_bytes=60 << 20),
    )(image_a, image_b, initial, coverage, seam_label)


def solution(mesh):
    placed = (P(None, "group", "blk"),) * 3 + (P("group", "blk"),) * 2
    return jax.shard_map(
        functools.partial(shards, mesh.shape["group"], mesh.shape["blk"]),
        mesh=mesh, in_specs=placed, out_specs=P(None, "group", "blk"), check_vma=False)
```

```python
import functools

import jax
import jax.numpy as jnp
from jax import lax
from jax.experimental import pallas as pl
from jax.experimental.pallas import tpu as pltpu
from jax.sharding import PartitionSpec as P

MESH = pl.DeviceIdType.MESH
F32 = jnp.float32
CHAN = 3
BS = 256
LANES = 128
HALO = 16
ROWS0 = BS + 2 * HALO + 16
ROWS1 = BS // 2 + HALO + 16
ROWS2 = BS // 4 + 2 * HALO + 16
ROWS3 = BS // 8 + HALO + 16
OWN0 = 8 + HALO
OWN1 = 16
OWN2 = 8 + HALO
OWN3 = 16
FROM_WEST = (0, 32, 64, 96, 16, 48)
FROM_EAST = tuple(at + 16 for at in FROM_WEST)
NEIGHBOURS = ((-1, 1), (-1, -1), (1, 1), (1, -1), (0, 1), (0, -1), (-1, 0), (1, 0))


def tile(base):
    return pl.ds(pl.multiple_of(base, 8), 8)


def sides(tiles, j, lane):
    n, here = len(tiles), tiles[j]
    after = here if n == 1 else jnp.where(lane == 0, tiles[(j + 1) % n], here)
    before = here if n == 1 else jnp.where(lane == LANES - 1, tiles[j - 1], here)
    return pltpu.roll(after, LANES - 1, 1) + pltpu.roll(before, 1, 1)


def beside(ref, slabs, base, lane, count=None):
    centre = [ref[s, tile(base), :] for s in slabs]
    around = []
    for j, s in enumerate(slabs[:count]):
        column = ref[s, pl.ds(base - 1, 8), :] + ref[s, pl.ds(base + 1, 8), :]
        around.append(column + sides(centre, j, lane))
    return centre, around


def take(x, index):
    return jnp.take_along_axis(x, index, axis=1)


def kernel(groups, blks, a_hbm, b_hbm, x_hbm, cov, lab, out,
           a_in, b_in, x_in, d, dh, pe, pw, hw, he, mask, labels,
           s0, v0, w0, s1, v1, w1, s2, pe2, pw2, hw2, he2, s2x, v2, w2, s3, v3, w3,
           in_sem, send1, recv1, send2, recv2):
    g, k = lax.axis_index("group"), lax.axis_index("blk")
    lane = lax.broadcasted_iota(jnp.int32, (8, LANES), 1)
    zeros = jnp.zeros((8, LANES), F32)

    spans = ((0, HALO), (BS - HALO, BS), (HALO, BS // 2), (BS // 2, BS - HALO))
    loads = [
        [
            pltpu.make_async_copy(src.at[:, lo:hi, :], dst.at[:, lo:hi, :], in_sem.at[n, i])
            for i, (src, dst) in enumerate(((a_hbm, a_in), (b_hbm, b_in), (x_hbm, x_in)))
        ]
        for n, (lo, hi) in enumerate(spans)
    ]
    for group in loads:
        for copy in group:
            copy.start()

    def there(dg, dk):
        ok = None
        for at, step, size in ((g, dg, groups), (k, dk, blks)):
            if step:
                good = at < size - 1 if step > 0 else at > 0
                ok = good if ok is None else jnp.logical_and(ok, good)
        return ok

    for slab in range(13):
        for base in (8, 16, BS + OWN0, BS + OWN0 + 8):
            d[slab, base:base + 8, :] = zeros
    for ref in (hw, he):
        @pl.loop(0, ROWS0 // 8, unroll=True)
        def _(i):
            ref[tile(8 * i), :] = zeros
    for ref in (hw2, he2):
        for base in range(0, ROWS2, 8):
            ref[base:base + 8, :] = zeros
    for c in range(CHAN):
        for base in (8, 16, BS // 4 + OWN2, BS // 4 + OWN2 + 8):
            s2[c, base:base + 8, :] = zeros
    for ref, rows in ((s0, ROWS0), (v0, ROWS0), (w0, ROWS0), (s1, ROWS1), (v1, ROWS1), (w1, ROWS1),
                      (s2x, ROWS2), (v2, ROWS2), (w2, ROWS2), (s3, ROWS3), (v3, ROWS3), (w3, ROWS3),
                      (d, ROWS0), (dh, ROWS0)):
        for slab in range(ref.shape[0]):
            ref[slab, 0:8, :] = zeros
            ref[slab, rows - 8:rows, :] = zeros

    barrier = pltpu.get_barrier_semaphore()
    count = jnp.int32(0)
    for dg, dk in NEIGHBOURS:
        ok = there(dg, dk)
        count = count + ok.astype(jnp.int32)

        @pl.when(ok)
        def _():
            pl.semaphore_signal(barrier, inc=1, device_id=(g + dg, k + dk), device_id_type=MESH)

    my_cov = jnp.full((8, LANES), cov[0, 0].astype(F32), F32)
    my_lab = jnp.full((8, LANES), lab[0, 0].astype(F32), F32)
    for base in (OWN0, BS + OWN0 - HALO):
        d[12, base:base + 8, :] = my_lab
        d[12, base + 8:base + 16, :] = my_cov
    meta_e = jnp.where(lane < 96, my_lab, my_cov)
    meta_w = jnp.where(lane < 96, my_lab, my_cov)

    def differences(i):
        rows, to = tile(8 * i), tile(OWN0 + 8 * i)
        right, left = meta_e, meta_w
        for c in range(CHAN):
            for t in range(2):
                cols = slice(LANES * t, LANES * (t + 1))
                x = x_in[c, rows, cols]
                for f, ref in enumerate((a_in, b_in)):
                    field = f * CHAN + c
                    diff = ref[c, rows, cols] - x
                    d[2 * field + t, to, :] = diff
                    start = FROM_WEST[field] if t else FROM_EAST[field]
                    here = jnp.logical_and(lane >= start, lane < start + 16)
                    if t == 0:
                        left = jnp.where(here, pltpu.roll(diff, start % LANES, 1), left)
                    else:
                        right = jnp.where(here, pltpu.roll(diff, (start + 16) % LANES, 1), right)
        pe[rows, :] = right
        pw[rows, :] = left

    def load_and_subtract(ns):
        for n in ns:
            for copy in loads[n]:
                copy.wait()
            pl.loop(spans[n][0] // 8, spans[n][1] // 8, unroll=True)(differences)

    def exchange(main, east, west, from_w, from_e, own, size, send, recv):
        n, top, low = HALO, own - HALO, own + size
        src_dst = {
            (-1, 1): (east.at[0:n], from_w.at[low:low + n]),
            (-1, -1): (west.at[0:n], from_e.at[low:low + n]),
            (1, 1): (east.at[size - n:size], from_w.at[top:top + n]),
            (1, -1): (west.at[size - n:size], from_e.at[top:top + n]),
            (0, 1): (east, from_w.at[own:own + size]),
            (0, -1): (west, from_e.at[own:own + size]),
            (-1, 0): (main.at[:, own:own + n, :], main.at[:, low:low + n, :]),
            (1, 0): (main.at[:, low - n:low, :], main.at[:, top:top + n, :]),
        }

        def copy_to(i, dg, dk):
            src, dst = src_dst[dg, dk]
            return pltpu.make_async_remote_copy(
                src_ref=src, dst_ref=dst, send_sem=send.at[i], recv_sem=recv.at[i],
                device_id=(g + dg, k + dk), device_id_type=MESH)

        def start(which):
            for i, (dg, dk) in enumerate(NEIGHBOURS):
                if (dg != 0) in which:
                    @pl.when(there(dg, dk))
                    def _():
                        copy_to(i, dg, dk).start()

        def finish():
            for i, (dg, dk) in enumerate(NEIGHBOURS):
                @pl.when(there(-dg, -dk))
                def _():
                    copy_to(i, dg, dk).wait_recv()
            for i, (dg, dk) in enumerate(NEIGHBOURS):
                @pl.when(there(dg, dk))
                def _():
                    copy_to(i, dg, dk).wait_send()

        return start, finish

    start, finish = exchange(d, pe, pw, hw, he, OWN0, BS, send1, recv1)
    load_and_subtract((0, 1))
    pl.semaphore_wait(barrier, count)
    start((True,))
    load_and_subtract((2, 3))
    start((False,))
    finish()

    for z, base in enumerate((8, OWN0, BS + OWN0)):
        west, east = hw[base:base + 8, :], he[base:base + 8, :]
        at = lambda where: jnp.full((8, LANES), where, jnp.int32)
        lab_w, cov_w = take(west, at(80)), take(west, at(112))
        lab_e, cov_e = take(east, at(0)), take(east, at(96))
        lab_z, cov_z = (my_lab, my_cov) if z == 1 else (d[12, base:base + 8, :], d[12, base + 8:base + 16, :])
        mask[z, 0] = cov_z
        mask[z, 1] = jnp.where(lane < 64, cov_e, cov_w)
        mask[z, 2] = jnp.where(lane < 64, cov_z, jnp.where(lane < 96, cov_e, cov_w))
        mask[z, 3] = jnp.where(lane < 32, cov_z, jnp.where(lane < 80, cov_e, cov_w))
        labels[z, 0] = lab_z
        labels[z, 1] = jnp.where(lane < 64, lab_e, lab_w)
        labels[z, 2] = jnp.where(lane < 64, lab_w, lab_e)

    def zone(i, before, own):
        return jnp.where(i < before, 0, jnp.where(i < before + own, 1, 2))

    @pl.loop(1, ROWS0 // 8 - 1, unroll=True)
    def _(i):
        west, east = hw[tile(8 * i), :], he[tile(8 * i), :]
        even = lax.rem(lane // 16, 2) == 0
        merged = jnp.where(even, west, east), jnp.where(even, east, west)
        for f in range(2 * CHAN):
            dh[f, tile(8 * i), :] = pltpu.roll(merged[f // 4], (112 - FROM_WEST[f]) % LANES, 1)

    def slabs0(c):
        return [3 * c, 3 * c + 1, 3 * c + 2]

    tiles0 = ROWS0 // 8 - 2

    @pl.loop(0, tiles0, unroll=True)
    def _(i):
        z = zone(i, 2, 32)
        base = 8 + 8 * i
        is_b = [labels[z, kind] == 1.0 for kind in range(3)]
        for c in range(CHAN):
            other = CHAN + c
            pairs = [(d.at[2 * c], d.at[2 * other]), (d.at[2 * c + 1], d.at[2 * other + 1]), (dh.at[c], dh.at[other])]

            def pick(t, kind, rows):
                return jnp.where(is_b[kind], pairs[t][1][rows, :], pairs[t][0][rows, :])

            for t in range(3):
                kind = t // 2
                centre = [pick(u, kind if kind == 0 or u == 2 else 2, tile(base)) for u in range(3)]
                column = pick(t, kind, pl.ds(base - 1, 8)) + pick(t, kind, pl.ds(base + 1, 8))
                s0[3 * c + t, tile(base), :] = mask[z, kind] * (
                    4.0 * centre[t] - (column + sides(centre, t, lane)))

    def down(s, v, w, tiles, zones, kinds, slabs_of, left_over, count=None):
        @pl.loop(0, tiles, unroll=True)
        def _(i):
            z, base = zone(i, *zones), 8 + 8 * i
            act = [mask[z, kind] * 0.04 for kind in sorted(set(kinds))]
            first = min(kinds)
            for c in range(CHAN):
                slabs = slabs_of(c)
                centre, around = beside(s, slabs, base, lane)
                for j, slab in enumerate(slabs):
                    v[slab, tile(base), :] = act[kinds[j] - first] * (6.0 * centre[j] + around[j])

        @pl.loop(*left_over, unroll=True)
        def _(i):
            z, base = zone(i, *zones), 8 + 8 * i
            for c in range(CHAN):
                slabs = slabs_of(c)
                centre, around = beside(v, slabs, base, lane, count)
                for j, slab in enumerate(slabs[:count]):
                    w[slab, tile(base), :] = mask[z, kinds[j]] * (
                        s[slab, tile(base), :] + (around[j] - 4.0 * centre[j]))

    def sweep(s, v, w, start, tiles, zones, kinds, slabs_of):
        @pl.loop(start, start + tiles, unroll=True)
        def _(i):
            z, base = zone(i, *zones), 8 + 8 * i
            act = [mask[z, kind] * 0.2 for kind in sorted(set(kinds))]
            first = min(kinds)
            for c in range(CHAN):
                slabs = slabs_of(c)
                centre, around = beside(v, slabs, base, lane)
                for j, slab in enumerate(slabs):
                    w[slab, tile(base), :] = act[kinds[j] - first] * (
                        centre[j] + around[j] + s[slab, tile(base), :])

    def add_rows(ref, slab, base):
        return ref[slab, pl.ds(base, 8, stride=2), :] + ref[slab, pl.ds(base + 1, 8, stride=2), :]

    def pair_rows(ref, slab, base):
        total = add_rows(ref, slab, base)
        return total + pltpu.roll(total, LANES - 1, 1)

    first = lax.rem(lane, 2) == 0
    interleaved = jnp.where(lane < 64, 2 * lane, 2 * lane - (LANES - 1))

    twice = lax.rem(2 * lane, LANES)
    low, high = lane // 2, lane // 2 + 64

    down(s0, v0, w0, tiles0, (2, 32), (0, 0, 1), slabs0, (1, tiles0 - 1))

    tiles1 = ROWS1 // 8 - 2

    def slabs1(c):
        return [2 * c, 2 * c + 1]

    @pl.loop(0, tiles1, unroll=True)
    def _(i):
        fine, base = 8 + 16 * i, 8 + 8 * i
        for c in range(CHAN):
            x, y = (add_rows(w0, 3 * c + t, fine) for t in range(2))
            pairs = jnp.where(first, x, pltpu.roll(y, 1, 1)) + jnp.where(first, pltpu.roll(x, LANES - 1, 1), y)
            s1[2 * c, tile(base), :] = take(pairs, interleaved)
            s1[2 * c + 1, tile(base), :] = take(pair_rows(w0, 3 * c + 2, fine), twice)

    down(s1, v1, w1, tiles1, (1, 16), (0, 1), slabs1, (1, tiles1 - 1), 1)

    @pl.loop(0, BS // 32, unroll=True)
    def _(i):
        right, left = zeros, zeros
        for c in range(CHAN):
            x = take(pair_rows(w1, 2 * c, OWN1 + 16 * i), twice)
            s2[c, tile(OWN2 + 8 * i), :] = x
            here = jnp.logical_and(lane >= 16 * c, lane < 16 * c + 16)
            left = jnp.where(here, pltpu.roll(x, 16 * c, 1), left)
            right = jnp.where(here, pltpu.roll(x, (16 * c - 48) % LANES, 1), right)
        pe2[tile(8 * i), :] = right
        pw2[tile(8 * i), :] = left

    start, finish = exchange(s2, pe2, pw2, hw2, he2, OWN2, BS // 4, send2, recv2)
    start((True, False))
    finish()

    tiles2 = ROWS2 // 8 - 2

    @pl.loop(0, tiles2, unroll=True)
    def _(i):
        rows = tile(8 + 8 * i)
        west, east = hw2[rows, :], he2[rows, :]
        for c in range(CHAN):
            side = jnp.where(lane < 80, pltpu.roll(east, (64 - 16 * c) % LANES, 1), 0.0)
            side = jnp.where(lane >= 112, pltpu.roll(west, 112 - 16 * c, 1), side)
            s2x[c, rows, :] = jnp.where(lane < 64, s2[c, rows, :], side)

    def slabs2(c):
        return [c]

    down(s2x, v2, w2, tiles2, (2, 8), (2,), slabs2, (0, tiles2))

    tiles3 = ROWS3 // 8 - 2

    @pl.loop(0, tiles3, unroll=True)
    def _(i):
        for c in range(CHAN):
            s3[c, tile(8 + 8 * i), :] = take(pair_rows(w2, c, 8 + 16 * i), twice)

    @pl.loop(0, tiles3, unroll=True)
    def _(i):
        z, base = zone(i, 1, 4), 8 + 8 * i
        for c in range(CHAN):
            (centre,), (around,) = beside(s3, [c], base, lane)
            v3[c, tile(base), :] = 0.04 * mask[z, 3] * (6.0 * centre + around)

    sweep(s3, v3, w3, 0, tiles3, (1, 4), (3,), slabs2)
    sweep(s3, w3, v3, 0, tiles3, (1, 4), (3,), slabs2)

    def add_up(v, slab, fine, act, value):
        for half in range(2):
            rows = pl.ds(fine + half, 8, stride=2)
            v[slab, rows, :] = v[slab, rows, :] + act * value

    @pl.loop(0, tiles3, unroll=True)
    def _(i):
        act = mask[zone(i, 1, 4), 2]
        for c in range(CHAN):
            value = v3[c, tile(8 + 8 * i), :]
            add_up(v2, c, 8 + 16 * i, act, take(value, jnp.where(lane < 96, low, high)))

    sweep(s2x, v2, w2, 0, tiles2, (2, 8), (2,), slabs2)
    sweep(s2x, w2, v2, 0, tiles2, (2, 8), (2,), slabs2)

    @pl.loop(0, ROWS1 // 16, unroll=True)
    def _(i):
        z = zone(i, 1, 8)
        for c in range(CHAN):
            value = v2[c, tile(OWN2 - 8 + 8 * i), :]
            add_up(v1, 2 * c, 16 * i, mask[z, 0], take(value, low))
            add_up(v1, 2 * c + 1, 16 * i, mask[z, 1], take(value, high))

    sweep(s1, v1, w1, 0, tiles1, (1, 16), (0, 1), slabs1)
    sweep(s1, w1, v1, 0, tiles1, (1, 16), (0, 1), slabs1)

    @pl.loop(0, tiles1, unroll=True)
    def _(i):
        z, fine = zone(i, 1, 16), 8 + 16 * i
        for c in range(CHAN):
            value, beyond = v1[2 * c, tile(8 + 8 * i), :], v1[2 * c + 1, tile(8 + 8 * i), :]
            add_up(v0, 3 * c, fine, mask[z, 0], take(value, low))
            add_up(v0, 3 * c + 1, fine, mask[z, 0], take(value, high))
            add_up(v0, 3 * c + 2, fine, mask[z, 1], take(beyond, jnp.where(lane < 64, low, high)))

    sweep(s0, v0, w0, 1, tiles0 - 2, (2, 32), (0, 0, 1), slabs0)

    act = mask[1, 0] * 0.2

    @pl.loop(0, BS // 8, unroll=True)
    def _(i):
        base = OWN0 + 8 * i
        for c in range(CHAN):
            centre, around = beside(w0, slabs0(c), base, lane, 2)
            for t in range(2):
                cols = slice(LANES * t, LANES * (t + 1))
                out[c, tile(8 * i), cols] = x_in[c, tile(8 * i), cols] + act * (
                    centre[t] + around[t] + s0[3 * c + t, tile(base), :])


def shards(groups, blks, image_a, image_b, initial, coverage, seam_label):
    vmem = lambda *dims: pltpu.VMEM(dims, F32)
    image = vmem(CHAN, BS, BS)
    scratch = [image] * 3
    scratch += [vmem(13, ROWS0, LANES), vmem(6, ROWS0, LANES)]
    scratch += [vmem(BS, LANES)] * 2 + [vmem(ROWS0, LANES)] * 2
    scratch += [vmem(3, 4, 8, LANES), vmem(3, 3, 8, LANES)]
    scratch += [vmem(9, ROWS0, LANES)] * 3 + [vmem(6, ROWS1, LANES)] * 3
    scratch += [vmem(3, ROWS2, LANES)] + [vmem(BS // 4, LANES)] * 2 + [vmem(ROWS2, LANES)] * 2
    scratch += [vmem(3, ROWS2, LANES)] * 3 + [vmem(3, ROWS3, LANES)] * 3
    scratch += [pltpu.SemaphoreType.DMA((4, 3))] + [pltpu.SemaphoreType.DMA((8,))] * 4
    return pl.pallas_call(
        functools.partial(kernel, groups, blks),
        out_shape=pltpu.VMEM(image_a.shape, F32),
        in_specs=[pl.BlockSpec(memory_space=pl.ANY)] * 3 + [pl.BlockSpec(memory_space=pltpu.SMEM)] * 2,
        out_specs=pl.BlockSpec(memory_space=pltpu.VMEM),
        scratch_shapes=scratch,
        compiler_params=pltpu.CompilerParams(
            collective_id=0, has_side_effects=True, vmem_limit_bytes=40 << 20),
    )(*(pltpu.with_memory_space_constraint(i, pltpu.HBM) for i in (image_a, image_b, initial)), coverage, seam_label)


def solution(mesh):
    placed = (P(None, "group", "blk"),) * 3 + (P("group", "blk"),) * 2
    return jax.shard_map(
        functools.partial(shards, mesh.shape["group"], mesh.shape["blk"]),
        mesh=mesh, in_specs=placed, out_specs=P(None, "group", "blk"), check_vma=False)
```

```python
import functools

import jax
import jax.numpy as jnp
from jax import lax
from jax.experimental import pallas as pl
from jax.experimental.pallas import tpu as pltpu
from jax.sharding import PartitionSpec as P

MESH = pl.DeviceIdType.MESH
F32 = jnp.float32
CHAN = 3
BS = 256
LANES = 128
SENT = 12
HALO = 16
ROWS0 = BS + 2 * HALO + 16
ROWS1 = BS // 2 + HALO + 16
ROWS2 = BS // 4 + 2 * HALO + 16
ROWS3 = BS // 8 + HALO + 16
OWN0 = 8 + HALO
OWN1 = 16
OWN2 = 8 + HALO
OWN3 = 16
FROM_WEST = (0, 32, 64, 96, 16, 48)
FROM_EAST = tuple(at + 16 for at in FROM_WEST)
NEIGHBOURS = ((-1, 1), (-1, -1), (1, 1), (1, -1), (0, 1), (0, -1), (-1, 0), (1, 0))


SENDS = ((-1, 1), (-1, -1), (1, 1), (1, -1), (-1, 0), (1, 0), (0, 1, 0), (0, -1, 0), (0, 1, 1), (0, -1, 1))


def tile(base):
    return pl.ds(pl.multiple_of(base, 8), 8)


def sides(tiles, j, lane):
    n, here = len(tiles), tiles[j]
    after = here if n == 1 else jnp.where(lane == 0, tiles[(j + 1) % n], here)
    before = here if n == 1 else jnp.where(lane == LANES - 1, tiles[j - 1], here)
    return pltpu.roll(after, LANES - 1, 1) + pltpu.roll(before, 1, 1)


def beside(ref, slabs, base, lane, count=None):
    centre = [ref[s, tile(base), :] for s in slabs]
    around = []
    for j, s in enumerate(slabs[:count]):
        column = ref[s, pl.ds(base - 1, 8), :] + ref[s, pl.ds(base + 1, 8), :]
        around.append(column + sides(centre, j, lane))
    return centre, around


def move(x, lanes):
    total = None
    for _ in range(3):
        part = x.astype(jnp.bfloat16)
        x = x - part.astype(F32)
        term = jnp.dot(part, lanes, preferred_element_type=F32)
        total = term if total is None else total + term
    return total


def ones_where(shape, test):
    k = lax.broadcasted_iota(jnp.int32, shape, 0)
    l = lax.broadcasted_iota(jnp.int32, shape, 1)
    return jnp.where(test(k, l), 1.0, 0.0).astype(jnp.bfloat16)


def kernel(groups, blks, a_hbm, b_hbm, x_hbm, cov, lab, out,
           a_in, b_in, x_in, d, dh, pe, pw, hw, he, mask, labels,
           s0, v0, w0, s1, v1, w1, s2, pe2, pw2, hw2, he2, s2x, v2, w2, s3, v3, w3,
           in_sem, send1, recv1, send2, recv2):
    g, k = lax.axis_index("group"), lax.axis_index("blk")
    lane = lax.broadcasted_iota(jnp.int32, (8, LANES), 1)
    zeros = jnp.zeros((8, LANES), F32)

    spans = ((0, HALO), (BS - HALO, BS), (HALO, BS // 2), (BS // 2, BS - HALO))
    loads = [
        [
            pltpu.make_async_copy(src.at[:, lo:hi, :], dst.at[:, lo:hi, :], in_sem.at[n, i])
            for i, (src, dst) in enumerate(((a_hbm, a_in), (b_hbm, b_in), (x_hbm, x_in)))
        ]
        for n, (lo, hi) in enumerate(spans)
    ]
    for group in loads:
        for copy in group:
            copy.start()

    def there(dg, dk):
        ok = None
        for at, step, size in ((g, dg, groups), (k, dk, blks)):
            if step:
                good = at < size - 1 if step > 0 else at > 0
                ok = good if ok is None else jnp.logical_and(ok, good)
        return ok

    for slab in range(13):
        for base in (8, 16, BS + OWN0, BS + OWN0 + 8):
            d[slab, base:base + 8, :] = zeros
    for ref in (hw, he):
        @pl.loop(0, ROWS0 // 8, unroll=True)
        def _(i):
            ref[tile(8 * i), :] = zeros
    for ref in (hw2, he2):
        for base in range(0, ROWS2, 8):
            ref[base:base + 8, :] = zeros
    for c in range(CHAN):
        for base in (8, 16, BS // 4 + OWN2, BS // 4 + OWN2 + 8):
            s2[c, base:base + 8, :] = zeros
    for ref, rows in ((s0, ROWS0), (v0, ROWS0), (w0, ROWS0), (s1, ROWS1), (v1, ROWS1), (w1, ROWS1),
                      (s2x, ROWS2), (v2, ROWS2), (w2, ROWS2), (s3, ROWS3), (v3, ROWS3), (w3, ROWS3),
                      (d, ROWS0), (dh, ROWS0)):
        for slab in range(ref.shape[0]):
            ref[slab, 0:8, :] = zeros
            ref[slab, rows - 8:rows, :] = zeros

    barrier = pltpu.get_barrier_semaphore()
    count = jnp.int32(0)
    for dg, dk in NEIGHBOURS:
        ok = there(dg, dk)
        count = count + ok.astype(jnp.int32)

        @pl.when(ok)
        def _():
            pl.semaphore_signal(barrier, inc=1, device_id=(g + dg, k + dk), device_id_type=MESH)

    my_cov = jnp.full((8, LANES), cov[0, 0].astype(F32), F32)
    my_lab = jnp.full((8, LANES), lab[0, 0].astype(F32), F32)
    for base in (OWN0, BS + OWN0 - HALO):
        d[12, base:base + 8, :] = my_lab
        d[12, base + 8:base + 16, :] = my_cov
    meta_e = jnp.where(lane < 96, my_lab, my_cov)
    meta_w = jnp.where(lane < 96, my_lab, my_cov)

    def differences(i):
        rows, to = tile(8 * i), tile(OWN0 + 8 * i)
        right, left = meta_e, meta_w
        for c in range(CHAN):
            for t in range(2):
                cols = slice(LANES * t, LANES * (t + 1))
                x = x_in[c, rows, cols]
                for f, ref in enumerate((a_in, b_in)):
                    field = f * CHAN + c
                    diff = ref[c, rows, cols] - x
                    d[2 * field + t, to, :] = diff
                    start = FROM_WEST[field] if t else FROM_EAST[field]
                    here = jnp.logical_and(lane >= start, lane < start + 16)
                    if t == 0:
                        left = jnp.where(here, pltpu.roll(diff, start % LANES, 1), left)
                    else:
                        right = jnp.where(here, pltpu.roll(diff, (start + 16) % LANES, 1), right)
        pe[rows, :] = right
        pw[rows, :] = left

    def load_and_subtract(ns):
        for n in ns:
            for copy in loads[n]:
                copy.wait()
            pl.loop(spans[n][0] // 8, spans[n][1] // 8, unroll=True)(differences)

    def exchange(main, east, west, from_w, from_e, own, size, send, recv):
        n, top, low = SENT, own - SENT, own + size
        src_dst = {
            (-1, 1): (east.at[0:n], from_w.at[low:low + n]),
            (-1, -1): (west.at[0:n], from_e.at[low:low + n]),
            (1, 1): (east.at[size - n:size], from_w.at[top:top + n]),
            (1, -1): (west.at[size - n:size], from_e.at[top:top + n]),
            (0, 1, 0): (east.at[0:size // 2], from_w.at[own:own + size // 2]),
            (0, 1, 1): (east.at[size // 2:size], from_w.at[own + size // 2:own + size]),
            (0, -1, 0): (west.at[0:size // 2], from_e.at[own:own + size // 2]),
            (0, -1, 1): (west.at[size // 2:size], from_e.at[own + size // 2:own + size]),
            (-1, 0): (main.at[:, own:own + n, :], main.at[:, low:low + n, :]),
            (1, 0): (main.at[:, low - n:low, :], main.at[:, top:top + n, :]),
        }

        def copy_to(i, dg, dk, *part):
            src, dst = src_dst[(dg, dk, *part)]
            return pltpu.make_async_remote_copy(
                src_ref=src, dst_ref=dst, send_sem=send.at[i], recv_sem=recv.at[i],
                device_id=(g + dg, k + dk), device_id_type=MESH)

        def start(which):
            for i in which:
                dg, dk, *part = SENDS[i]

                @pl.when(there(dg, dk))
                def _():
                    copy_to(i, dg, dk, *part).start()

        def finish():
            for i, (dg, dk, *part) in enumerate(SENDS):
                @pl.when(there(-dg, -dk))
                def _():
                    copy_to(i, dg, dk, *part).wait_recv()
            for i, (dg, dk, *part) in enumerate(SENDS):
                @pl.when(there(dg, dk))
                def _():
                    copy_to(i, dg, dk, *part).wait_send()

        return start, finish

    start, finish = exchange(d, pe, pw, hw, he, OWN0, BS, send1, recv1)
    load_and_subtract((0, 1))
    pl.semaphore_wait(barrier, count)
    start(range(6))
    load_and_subtract((2,))
    start((6, 7))
    load_and_subtract((3,))
    start((8, 9))
    finish()

    for z, base in enumerate((8, OWN0, BS + OWN0)):
        at_row = base + 8 if z == 0 else base
        west, east = hw[at_row:at_row + 8, :], he[at_row:at_row + 8, :]
        at = lambda x, where: jnp.broadcast_to(x[:, where:where + 1], (8, LANES))
        lab_w, cov_w = at(west, 80), at(west, 112)
        lab_e, cov_e = at(east, 0), at(east, 96)
        lab_z, cov_z = (my_lab, my_cov) if z == 1 else tuple(
            jnp.broadcast_to(d[12, row:row + 1, :], (8, LANES)) for row in (base + 7, base + 8))
        mask[z, 0] = cov_z
        mask[z, 1] = jnp.where(lane < 64, cov_e, cov_w)
        mask[z, 2] = jnp.where(lane < 64, cov_z, jnp.where(lane < 96, cov_e, cov_w))
        mask[z, 3] = jnp.where(lane < 32, cov_z, jnp.where(lane < 80, cov_e, cov_w))
        labels[z, 0] = lab_z
        labels[z, 1] = jnp.where(lane < 64, lab_e, lab_w)
        labels[z, 2] = jnp.where(lane < 64, lab_w, lab_e)

    def zone(i, before, own):
        return jnp.where(i < before, 0, jnp.where(i < before + own, 1, 2))

    @pl.loop(1, ROWS0 // 8 - 1, unroll=True)
    def _(i):
        west, east = hw[tile(8 * i), :], he[tile(8 * i), :]
        even = lax.rem(lane // 16, 2) == 0
        merged = jnp.where(even, west, east), jnp.where(even, east, west)
        for f in range(2 * CHAN):
            dh[f, tile(8 * i), :] = pltpu.roll(merged[f // 4], (112 - FROM_WEST[f]) % LANES, 1)

    def slabs0(c):
        return [3 * c, 3 * c + 1, 3 * c + 2]

    tiles0 = ROWS0 // 8 - 2

    @pl.loop(0, tiles0, unroll=True)
    def _(i):
        z = zone(i, 2, 32)
        base = 8 + 8 * i
        is_b = [labels[z, kind] == 1.0 for kind in range(3)]
        for c in range(CHAN):
            other = CHAN + c
            pairs = [(d.at[2 * c], d.at[2 * other]), (d.at[2 * c + 1], d.at[2 * other + 1]), (dh.at[c], dh.at[other])]

            def pick(t, kind, rows):
                return jnp.where(is_b[kind], pairs[t][1][rows, :], pairs[t][0][rows, :])

            for t in range(3):
                kind = t // 2
                centre = [pick(u, kind if kind == 0 or u == 2 else 2, tile(base)) for u in range(3)]
                column = pick(t, kind, pl.ds(base - 1, 8)) + pick(t, kind, pl.ds(base + 1, 8))
                s0[3 * c + t, tile(base), :] = mask[z, kind] * (
                    4.0 * centre[t] - (column + sides(centre, t, lane)))

    def down(s, v, w, tiles, zones, kinds, slabs_of, left_over, count=None):
        @pl.loop(0, tiles, unroll=True)
        def _(i):
            z, base = zone(i, *zones), 8 + 8 * i
            act = [mask[z, kind] * 0.04 for kind in sorted(set(kinds))]
            first = min(kinds)
            for c in range(CHAN):
                slabs = slabs_of(c)
                centre, around = beside(s, slabs, base, lane)
                for j, slab in enumerate(slabs):
                    v[slab, tile(base), :] = act[kinds[j] - first] * (6.0 * centre[j] + around[j])

        @pl.loop(*left_over, unroll=True)
        def _(i):
            z, base = zone(i, *zones), 8 + 8 * i
            for c in range(CHAN):
                slabs = slabs_of(c)
                centre, around = beside(v, slabs, base, lane, count)
                for j, slab in enumerate(slabs[:count]):
                    w[slab, tile(base), :] = mask[z, kinds[j]] * (
                        s[slab, tile(base), :] + (around[j] - 4.0 * centre[j]))

    def sweep(s, v, w, start, tiles, zones, kinds, slabs_of):
        @pl.loop(start, start + tiles, unroll=True)
        def _(i):
            z, base = zone(i, *zones), 8 + 8 * i
            act = [mask[z, kind] * 0.2 for kind in sorted(set(kinds))]
            first = min(kinds)
            for c in range(CHAN):
                slabs = slabs_of(c)
                centre, around = beside(v, slabs, base, lane)
                for j, slab in enumerate(slabs):
                    w[slab, tile(base), :] = act[kinds[j] - first] * (
                        centre[j] + around[j] + s[slab, tile(base), :])

    def add_rows(ref, slab, base, rows):
        return ref[slab, pl.ds(base, rows, stride=2), :] + ref[slab, pl.ds(base + 1, rows, stride=2), :]

    square = (LANES, LANES)
    halve = ones_where((2 * LANES, LANES), lambda k, l: k // 2 == l)
    halve_one = ones_where(square, lambda k, l: k // 2 == lax.rem(l, 64))
    double = ones_where((LANES, 2 * LANES), lambda k, l: k == l // 2)
    double_sides = ones_where(square, lambda k, l: k == jnp.where(l < 64, l // 2, l // 2 + 64))
    double_coarse = ones_where(square, lambda k, l: k == jnp.where(l < 96, l // 2, l // 2 + 64))

    down(s0, v0, w0, tiles0, (2, 32), (0, 0, 1), slabs0, (1, tiles0 - 1))

    tiles1 = ROWS1 // 8 - 2

    def slabs1(c):
        return [2 * c, 2 * c + 1]

    rows1 = 8 * tiles1
    for c in range(CHAN):
        middle = jnp.concatenate([add_rows(w0, 3 * c + t, 8, rows1) for t in range(2)], axis=1)
        s1[2 * c, 8:8 + rows1, :] = move(middle, halve)
        s1[2 * c + 1, 8:8 + rows1, :] = move(add_rows(w0, 3 * c + 2, 8, rows1), halve_one)

    down(s1, v1, w1, tiles1, (1, 16), (0, 1), slabs1, (1, tiles1 - 1), 1)

    for c in range(CHAN):
        s2[c, OWN2:OWN2 + BS // 4, :] = move(add_rows(w1, 2 * c, OWN1, BS // 4), halve_one)

    @pl.loop(0, BS // 32, unroll=True)
    def _(i):
        right, left = zeros, zeros
        for c in range(CHAN):
            x = s2[c, tile(OWN2 + 8 * i), :]
            here = jnp.logical_and(lane >= 16 * c, lane < 16 * c + 16)
            left = jnp.where(here, pltpu.roll(x, 16 * c, 1), left)
            right = jnp.where(here, pltpu.roll(x, (16 * c - 48) % LANES, 1), right)
        pe2[tile(8 * i), :] = right
        pw2[tile(8 * i), :] = left

    start, finish = exchange(s2, pe2, pw2, hw2, he2, OWN2, BS // 4, send2, recv2)
    start(range(10))
    finish()

    tiles2 = ROWS2 // 8 - 2

    @pl.loop(0, tiles2, unroll=True)
    def _(i):
        rows = tile(8 + 8 * i)
        west, east = hw2[rows, :], he2[rows, :]
        for c in range(CHAN):
            side = jnp.where(lane < 80, pltpu.roll(east, (64 - 16 * c) % LANES, 1), 0.0)
            side = jnp.where(lane >= 112, pltpu.roll(west, 112 - 16 * c, 1), side)
            s2x[c, rows, :] = jnp.where(lane < 64, s2[c, rows, :], side)

    def slabs2(c):
        return [c]

    down(s2x, v2, w2, tiles2, (2, 8), (2,), slabs2, (0, tiles2))

    tiles3 = ROWS3 // 8 - 2

    rows3 = 8 * tiles3
    for c in range(CHAN):
        s3[c, 8:8 + rows3, :] = move(add_rows(w2, c, 8, rows3), halve_one)

    @pl.loop(0, tiles3, unroll=True)
    def _(i):
        z, base = zone(i, 1, 4), 8 + 8 * i
        for c in range(CHAN):
            (centre,), (around,) = beside(s3, [c], base, lane)
            v3[c, tile(base), :] = 0.04 * mask[z, 3] * (6.0 * centre + around)

    sweep(s3, v3, w3, 0, tiles3, (1, 4), (3,), slabs2)
    sweep(s3, w3, v3, 0, tiles3, (1, 4), (3,), slabs2)

    def add_up(v, slab, fine, act, value):
        for half in range(2):
            rows = pl.ds(fine + half, 8, stride=2)
            v[slab, rows, :] = v[slab, rows, :] + act * value

    for c in range(CHAN):
        w3[c, 8:8 + rows3, :] = move(v3[c, 8:8 + rows3, :], double_coarse)

    @pl.loop(0, tiles3, unroll=True)
    def _(i):
        act = mask[zone(i, 1, 4), 2]
        for c in range(CHAN):
            add_up(v2, c, 8 + 16 * i, act, w3[c, tile(8 + 8 * i), :])

    sweep(s2x, v2, w2, 0, tiles2, (2, 8), (2,), slabs2)
    sweep(s2x, w2, v2, 0, tiles2, (2, 8), (2,), slabs2)

    half1 = ROWS1 // 2
    for c in range(CHAN):
        both = move(v2[c, OWN2 - 8:OWN2 - 8 + half1, :], double)
        for t in range(2):
            w1[2 * c + t, 0:half1, :] = both[:, LANES * t:LANES * (t + 1)]

    @pl.loop(0, ROWS1 // 16, unroll=True)
    def _(i):
        z = zone(i, 1, 8)
        for c in range(CHAN):
            for t in range(2):
                add_up(v1, 2 * c + t, 16 * i, mask[z, t], w1[2 * c + t, tile(8 * i), :])

    sweep(s1, v1, w1, 0, tiles1, (1, 16), (0, 1), slabs1)
    sweep(s1, w1, v1, 0, tiles1, (1, 16), (0, 1), slabs1)

    for c in range(CHAN):
        both = move(v1[2 * c, 8:8 + rows1, :], double)
        for t in range(2):
            w0[3 * c + t, 8:8 + rows1, :] = both[:, LANES * t:LANES * (t + 1)]
        w0[3 * c + 2, 8:8 + rows1, :] = move(v1[2 * c + 1, 8:8 + rows1, :], double_sides)

    @pl.loop(0, tiles1, unroll=True)
    def _(i):
        z = zone(i, 1, 16)
        for c in range(CHAN):
            for t in range(3):
                add_up(v0, 3 * c + t, 8 + 16 * i, mask[z, t // 2], w0[3 * c + t, tile(8 + 8 * i), :])

    sweep(s0, v0, w0, 1, tiles0 - 2, (2, 32), (0, 0, 1), slabs0)

    act = mask[1, 0] * 0.2

    @pl.loop(0, BS // 8, unroll=True)
    def _(i):
        base = OWN0 + 8 * i
        for c in range(CHAN):
            centre, around = beside(w0, slabs0(c), base, lane, 2)
            for t in range(2):
                cols = slice(LANES * t, LANES * (t + 1))
                out[c, tile(8 * i), cols] = x_in[c, tile(8 * i), cols] + act * (
                    centre[t] + around[t] + s0[3 * c + t, tile(base), :])


def shards(groups, blks, image_a, image_b, initial, coverage, seam_label):
    vmem = lambda *dims: pltpu.VMEM(dims, F32)
    image = vmem(CHAN, BS, BS)
    scratch = [image] * 3
    scratch += [vmem(13, ROWS0, LANES), vmem(6, ROWS0, LANES)]
    scratch += [vmem(BS, LANES)] * 2 + [vmem(ROWS0, LANES)] * 2
    scratch += [vmem(3, 4, 8, LANES), vmem(3, 3, 8, LANES)]
    scratch += [vmem(9, ROWS0, LANES)] * 3 + [vmem(6, ROWS1, LANES)] * 3
    scratch += [vmem(3, ROWS2, LANES)] + [vmem(BS // 4, LANES)] * 2 + [vmem(ROWS2, LANES)] * 2
    scratch += [vmem(3, ROWS2, LANES)] * 3 + [vmem(3, ROWS3, LANES)] * 3
    scratch += [pltpu.SemaphoreType.DMA((4, 3))] + [pltpu.SemaphoreType.DMA((len(SENDS),))] * 4
    return pl.pallas_call(
        functools.partial(kernel, groups, blks),
        out_shape=pltpu.VMEM(image_a.shape, F32),
        in_specs=[pl.BlockSpec(memory_space=pl.ANY)] * 3 + [pl.BlockSpec(memory_space=pltpu.SMEM)] * 2,
        out_specs=pl.BlockSpec(memory_space=pltpu.VMEM),
        scratch_shapes=scratch,
        compiler_params=pltpu.CompilerParams(
            collective_id=0, has_side_effects=True, vmem_limit_bytes=40 << 20),
    )(*(pltpu.with_memory_space_constraint(i, pltpu.HBM) for i in (image_a, image_b, initial)), coverage, seam_label)


def solution(mesh):
    placed = (P(None, "group", "blk"),) * 3 + (P("group", "blk"),) * 2
    return jax.shard_map(
        functools.partial(shards, mesh.shape["group"], mesh.shape["blk"]),
        mesh=mesh, in_specs=placed, out_specs=P(None, "group", "blk"), check_vma=False)
```

```python
import functools

import jax
import jax.numpy as jnp
from jax import lax
from jax.experimental import pallas as pl
from jax.experimental.pallas import tpu as pltpu
from jax.sharding import PartitionSpec as P

MESH = pl.DeviceIdType.MESH
F32 = jnp.float32
CHAN = 3
BS = 256
LANES = 128
SENT = 12
HALO = 16
ROWS0 = BS + 2 * HALO + 16
ROWS1 = BS // 2 + HALO + 16
ROWS2 = BS // 4 + 2 * HALO + 16
ROWS3 = BS // 8 + HALO + 16
OWN0 = 8 + HALO
OWN1 = 16
OWN2 = 8 + HALO
OWN3 = 16
FROM_WEST = (0, 32, 64, 96, 16, 48)
FROM_EAST = tuple(at + 16 for at in FROM_WEST)
NEIGHBOURS = ((-1, 1), (-1, -1), (1, 1), (1, -1), (0, 1), (0, -1), (-1, 0), (1, 0))


SENDS = ((-1, 1), (-1, -1), (1, 1), (1, -1), (-1, 0), (1, 0), (0, 1, 0), (0, -1, 0), (0, 1, 1), (0, -1, 1))


def tile(base):
    return pl.ds(pl.multiple_of(base, 8), 8)


def sides(tiles, j, lane):
    n, here = len(tiles), tiles[j]
    after = here if n == 1 else jnp.where(lane == 0, tiles[(j + 1) % n], here)
    before = here if n == 1 else jnp.where(lane == LANES - 1, tiles[j - 1], here)
    return pltpu.roll(after, LANES - 1, 1) + pltpu.roll(before, 1, 1)


def beside(ref, slabs, base, lane, count=None):
    centre = [ref[s, tile(base), :] for s in slabs]
    around = []
    for j, s in enumerate(slabs[:count]):
        column = ref[s, pl.ds(base - 1, 8), :] + ref[s, pl.ds(base + 1, 8), :]
        around.append(column + sides(centre, j, lane))
    return centre, around


def move(x, lanes):
    total = None
    for _ in range(3):
        part = x.astype(jnp.bfloat16)
        x = x - part.astype(F32)
        term = jnp.dot(part, lanes, preferred_element_type=F32)
        total = term if total is None else total + term
    return total


def ones_where(shape, test):
    k = lax.broadcasted_iota(jnp.int32, shape, 0)
    l = lax.broadcasted_iota(jnp.int32, shape, 1)
    return jnp.where(test(k, l), 1.0, 0.0).astype(jnp.bfloat16)


def kernel(groups, blks, a_hbm, b_hbm, x_hbm, cov, lab, out,
           a_in, b_in, x_in, d, dh, pe, pw, hw, he, mask, labels,
           s0, v0, w0, s1, v1, w1, s2, pe2, pw2, hw2, he2, s2x, v2, w2, s3, v3, w3,
           in_sem, send1, recv1, send2, recv2):
    g, k = lax.axis_index("group"), lax.axis_index("blk")
    lane = lax.broadcasted_iota(jnp.int32, (8, LANES), 1)
    zeros = jnp.zeros((8, LANES), F32)

    spans = ((0, HALO), (BS - HALO, BS), (HALO, BS // 2), (BS // 2, BS - HALO))
    loads = [
        [
            pltpu.make_async_copy(src.at[:, lo:hi, :], dst.at[:, lo:hi, :], in_sem.at[n, i])
            for i, (src, dst) in enumerate(((a_hbm, a_in), (b_hbm, b_in), (x_hbm, x_in)))
        ]
        for n, (lo, hi) in enumerate(spans)
    ]
    for group in loads:
        for copy in group:
            copy.start()

    def there(dg, dk):
        ok = None
        for at, step, size in ((g, dg, groups), (k, dk, blks)):
            if step:
                good = at < size - 1 if step > 0 else at > 0
                ok = good if ok is None else jnp.logical_and(ok, good)
        return ok

    for slab in range(13):
        for base in (8, 16, BS + OWN0, BS + OWN0 + 8):
            d[slab, base:base + 8, :] = zeros
    for ref in (hw, he):
        @pl.loop(0, ROWS0 // 8, unroll=True)
        def _(i):
            ref[tile(8 * i), :] = zeros
    for ref in (hw2, he2):
        for base in range(0, ROWS2, 8):
            ref[base:base + 8, :] = zeros
    for c in range(CHAN):
        for base in (8, 16, BS // 4 + OWN2, BS // 4 + OWN2 + 8):
            s2[c, base:base + 8, :] = zeros
    barrier = pltpu.get_barrier_semaphore()
    count = jnp.int32(0)
    for dg, dk in NEIGHBOURS:
        ok = there(dg, dk)
        count = count + ok.astype(jnp.int32)

        @pl.when(ok)
        def _():
            pl.semaphore_signal(barrier, inc=1, device_id=(g + dg, k + dk), device_id_type=MESH)

    for ref, rows in ((s0, ROWS0), (v0, ROWS0), (w0, ROWS0), (s1, ROWS1), (v1, ROWS1), (w1, ROWS1),
                      (s2x, ROWS2), (v2, ROWS2), (w2, ROWS2), (s3, ROWS3), (v3, ROWS3), (w3, ROWS3),
                      (d, ROWS0), (dh, ROWS0)):
        for slab in range(ref.shape[0]):
            ref[slab, 0:8, :] = zeros
            ref[slab, rows - 8:rows, :] = zeros

    my_cov = jnp.full((8, LANES), cov[0, 0].astype(F32), F32)
    my_lab = jnp.full((8, LANES), lab[0, 0].astype(F32), F32)
    for base in (OWN0, BS + OWN0 - HALO):
        d[12, base:base + 8, :] = my_lab
        d[12, base + 8:base + 16, :] = my_cov
    meta_e = jnp.where(lane < 96, my_lab, my_cov)
    meta_w = jnp.where(lane < 96, my_lab, my_cov)

    def differences(i):
        rows, to = tile(8 * i), tile(OWN0 + 8 * i)
        right, left = meta_e, meta_w
        for c in range(CHAN):
            for t in range(2):
                cols = slice(LANES * t, LANES * (t + 1))
                x = x_in[c, rows, cols]
                for f, ref in enumerate((a_in, b_in)):
                    field = f * CHAN + c
                    diff = ref[c, rows, cols] - x
                    d[2 * field + t, to, :] = diff
                    start = FROM_WEST[field] if t else FROM_EAST[field]
                    here = jnp.logical_and(lane >= start, lane < start + 16)
                    if t == 0:
                        left = jnp.where(here, pltpu.roll(diff, start % LANES, 1), left)
                    else:
                        right = jnp.where(here, pltpu.roll(diff, (start + 16) % LANES, 1), right)
        pe[rows, :] = right
        pw[rows, :] = left

    def load_and_subtract(ns):
        for n in ns:
            for copy in loads[n]:
                copy.wait()
            pl.loop(spans[n][0] // 8, spans[n][1] // 8, unroll=True)(differences)

    def exchange(main, east, west, from_w, from_e, own, size, send, recv):
        n, top, low = SENT, own - SENT, own + size
        src_dst = {
            (-1, 1): (east.at[0:n], from_w.at[low:low + n]),
            (-1, -1): (west.at[0:n], from_e.at[low:low + n]),
            (1, 1): (east.at[size - n:size], from_w.at[top:top + n]),
            (1, -1): (west.at[size - n:size], from_e.at[top:top + n]),
            (0, 1, 0): (east.at[0:size // 2], from_w.at[own:own + size // 2]),
            (0, 1, 1): (east.at[size // 2:size], from_w.at[own + size // 2:own + size]),
            (0, -1, 0): (west.at[0:size // 2], from_e.at[own:own + size // 2]),
            (0, -1, 1): (west.at[size // 2:size], from_e.at[own + size // 2:own + size]),
            (-1, 0): (main.at[:, own:own + n, :], main.at[:, low:low + n, :]),
            (1, 0): (main.at[:, low - n:low, :], main.at[:, top:top + n, :]),
        }

        def copy_to(i, dg, dk, *part):
            src, dst = src_dst[(dg, dk, *part)]
            return pltpu.make_async_remote_copy(
                src_ref=src, dst_ref=dst, send_sem=send.at[i], recv_sem=recv.at[i],
                device_id=(g + dg, k + dk), device_id_type=MESH)

        def start(which):
            for i in which:
                dg, dk, *part = SENDS[i]

                @pl.when(there(dg, dk))
                def _():
                    copy_to(i, dg, dk, *part).start()

        def finish():
            for i, (dg, dk, *part) in enumerate(SENDS):
                @pl.when(there(-dg, -dk))
                def _():
                    copy_to(i, dg, dk, *part).wait_recv()

        def sent():
            for i, (dg, dk, *part) in enumerate(SENDS):
                @pl.when(there(dg, dk))
                def _():
                    copy_to(i, dg, dk, *part).wait_send()

        return start, finish, sent

    start, finish, sent = exchange(d, pe, pw, hw, he, OWN0, BS, send1, recv1)
    load_and_subtract((0, 1))
    pl.semaphore_wait(barrier, count)
    start(range(6))
    load_and_subtract((2,))
    start((6, 7))
    load_and_subtract((3,))
    start((8, 9))
    finish()

    for z, base in enumerate((8, OWN0, BS + OWN0)):
        at_row = base + 8 if z == 0 else base
        west, east = hw[at_row:at_row + 8, :], he[at_row:at_row + 8, :]
        at = lambda x, where: jnp.broadcast_to(x[:, where:where + 1], (8, LANES))
        lab_w, cov_w = at(west, 80), at(west, 112)
        lab_e, cov_e = at(east, 0), at(east, 96)
        lab_z, cov_z = (my_lab, my_cov) if z == 1 else tuple(
            jnp.broadcast_to(d[12, row:row + 1, :], (8, LANES)) for row in (base + 7, base + 8))
        mask[z, 0] = cov_z
        mask[z, 1] = jnp.where(lane < 64, cov_e, cov_w)
        mask[z, 2] = jnp.where(lane < 64, cov_z, jnp.where(lane < 96, cov_e, cov_w))
        mask[z, 3] = jnp.where(lane < 32, cov_z, jnp.where(lane < 80, cov_e, cov_w))
        labels[z, 0] = lab_z
        labels[z, 1] = jnp.where(lane < 64, lab_e, lab_w)
        labels[z, 2] = jnp.where(lane < 64, lab_w, lab_e)

    def zone(i, before, own):
        return jnp.where(i < before, 0, jnp.where(i < before + own, 1, 2))

    @pl.loop(1, ROWS0 // 8 - 1, unroll=True)
    def _(i):
        west, east = hw[tile(8 * i), :], he[tile(8 * i), :]
        even = lax.rem(lane // 16, 2) == 0
        merged = jnp.where(even, west, east), jnp.where(even, east, west)
        for f in range(2 * CHAN):
            dh[f, tile(8 * i), :] = pltpu.roll(merged[f // 4], (112 - FROM_WEST[f]) % LANES, 1)

    def slabs0(c):
        return [3 * c, 3 * c + 1, 3 * c + 2]

    tiles0 = ROWS0 // 8 - 2

    @pl.loop(0, tiles0, unroll=True)
    def _(i):
        z = zone(i, 2, 32)
        base = 8 + 8 * i
        is_b = [labels[z, kind] == 1.0 for kind in range(3)]
        for c in range(CHAN):
            other = CHAN + c
            pairs = [(d.at[2 * c], d.at[2 * other]), (d.at[2 * c + 1], d.at[2 * other + 1]), (dh.at[c], dh.at[other])]

            def pick(t, kind, rows):
                return jnp.where(is_b[kind], pairs[t][1][rows, :], pairs[t][0][rows, :])

            for t in range(3):
                kind = t // 2
                centre = [pick(u, kind if kind == 0 or u == 2 else 2, tile(base)) for u in range(3)]
                column = pick(t, kind, pl.ds(base - 1, 8)) + pick(t, kind, pl.ds(base + 1, 8))
                s0[3 * c + t, tile(base), :] = mask[z, kind] * (
                    4.0 * centre[t] - (column + sides(centre, t, lane)))

    def down(s, v, w, tiles, zones, kinds, slabs_of, left_over, count=None):
        @pl.loop(0, tiles, unroll=True)
        def _(i):
            z, base = zone(i, *zones), 8 + 8 * i
            act = [mask[z, kind] * 0.04 for kind in sorted(set(kinds))]
            first = min(kinds)
            for c in range(CHAN):
                slabs = slabs_of(c)
                centre, around = beside(s, slabs, base, lane)
                for j, slab in enumerate(slabs):
                    v[slab, tile(base), :] = act[kinds[j] - first] * (6.0 * centre[j] + around[j])

        @pl.loop(*left_over, unroll=True)
        def _(i):
            z, base = zone(i, *zones), 8 + 8 * i
            for c in range(CHAN):
                slabs = slabs_of(c)
                centre, around = beside(v, slabs, base, lane, count)
                for j, slab in enumerate(slabs[:count]):
                    w[slab, tile(base), :] = mask[z, kinds[j]] * (
                        s[slab, tile(base), :] + (around[j] - 4.0 * centre[j]))

    def sweep(s, v, w, start, tiles, zones, kinds, slabs_of):
        @pl.loop(start, start + tiles, unroll=True)
        def _(i):
            z, base = zone(i, *zones), 8 + 8 * i
            act = [mask[z, kind] * 0.2 for kind in sorted(set(kinds))]
            first = min(kinds)
            for c in range(CHAN):
                slabs = slabs_of(c)
                centre, around = beside(v, slabs, base, lane)
                for j, slab in enumerate(slabs):
                    w[slab, tile(base), :] = act[kinds[j] - first] * (
                        centre[j] + around[j] + s[slab, tile(base), :])

    def add_rows(ref, slab, base, rows):
        return ref[slab, pl.ds(base, rows, stride=2), :] + ref[slab, pl.ds(base + 1, rows, stride=2), :]

    square = (LANES, LANES)
    halve = ones_where((2 * LANES, LANES), lambda k, l: k // 2 == l)
    halve_one = ones_where(square, lambda k, l: k // 2 == lax.rem(l, 64))
    double = ones_where((LANES, 2 * LANES), lambda k, l: k == l // 2)
    double_sides = ones_where(square, lambda k, l: k == jnp.where(l < 64, l // 2, l // 2 + 64))
    double_coarse = ones_where(square, lambda k, l: k == jnp.where(l < 96, l // 2, l // 2 + 64))

    down(s0, v0, w0, tiles0, (2, 32), (0, 0, 1), slabs0, (1, tiles0 - 1))

    tiles1 = ROWS1 // 8 - 2

    def slabs1(c):
        return [2 * c, 2 * c + 1]

    rows1 = 8 * tiles1
    for c in range(CHAN):
        middle = jnp.concatenate([add_rows(w0, 3 * c + t, 8, rows1) for t in range(2)], axis=1)
        s1[2 * c, 8:8 + rows1, :] = move(middle, halve)
        s1[2 * c + 1, 8:8 + rows1, :] = move(add_rows(w0, 3 * c + 2, 8, rows1), halve_one)

    down(s1, v1, w1, tiles1, (1, 16), (0, 1), slabs1, (1, tiles1 - 1), 1)

    for c in range(CHAN):
        s2[c, OWN2:OWN2 + BS // 4, :] = move(add_rows(w1, 2 * c, OWN1, BS // 4), halve_one)

    @pl.loop(0, BS // 32, unroll=True)
    def _(i):
        right, left = zeros, zeros
        for c in range(CHAN):
            x = s2[c, tile(OWN2 + 8 * i), :]
            here = jnp.logical_and(lane >= 16 * c, lane < 16 * c + 16)
            left = jnp.where(here, pltpu.roll(x, 16 * c, 1), left)
            right = jnp.where(here, pltpu.roll(x, (16 * c - 48) % LANES, 1), right)
        pe2[tile(8 * i), :] = right
        pw2[tile(8 * i), :] = left

    start, finish, sent_too = exchange(s2, pe2, pw2, hw2, he2, OWN2, BS // 4, send2, recv2)
    start(range(10))
    finish()

    tiles2 = ROWS2 // 8 - 2

    @pl.loop(0, tiles2, unroll=True)
    def _(i):
        rows = tile(8 + 8 * i)
        west, east = hw2[rows, :], he2[rows, :]
        for c in range(CHAN):
            side = jnp.where(lane < 80, pltpu.roll(east, (64 - 16 * c) % LANES, 1), 0.0)
            side = jnp.where(lane >= 112, pltpu.roll(west, 112 - 16 * c, 1), side)
            s2x[c, rows, :] = jnp.where(lane < 64, s2[c, rows, :], side)

    def slabs2(c):
        return [c]

    down(s2x, v2, w2, tiles2, (2, 8), (2,), slabs2, (0, tiles2))

    tiles3 = ROWS3 // 8 - 2

    rows3 = 8 * tiles3
    for c in range(CHAN):
        s3[c, 8:8 + rows3, :] = move(add_rows(w2, c, 8, rows3), halve_one)

    @pl.loop(0, tiles3, unroll=True)
    def _(i):
        z, base = zone(i, 1, 4), 8 + 8 * i
        for c in range(CHAN):
            (centre,), (around,) = beside(s3, [c], base, lane)
            v3[c, tile(base), :] = 0.04 * mask[z, 3] * (6.0 * centre + around)

    sweep(s3, v3, w3, 0, tiles3, (1, 4), (3,), slabs2)
    sweep(s3, w3, v3, 0, tiles3, (1, 4), (3,), slabs2)

    def add_up(v, slab, fine, act, value):
        for half in range(2):
            rows = pl.ds(fine + half, 8, stride=2)
            v[slab, rows, :] = v[slab, rows, :] + act * value

    for c in range(CHAN):
        w3[c, 8:8 + rows3, :] = move(v3[c, 8:8 + rows3, :], double_coarse)

    @pl.loop(0, tiles3, unroll=True)
    def _(i):
        act = mask[zone(i, 1, 4), 2]
        for c in range(CHAN):
            add_up(v2, c, 8 + 16 * i, act, w3[c, tile(8 + 8 * i), :])

    sweep(s2x, v2, w2, 0, tiles2, (2, 8), (2,), slabs2)
    sweep(s2x, w2, v2, 0, tiles2, (2, 8), (2,), slabs2)

    half1 = ROWS1 // 2
    for c in range(CHAN):
        both = move(v2[c, OWN2 - 8:OWN2 - 8 + half1, :], double)
        for t in range(2):
            w1[2 * c + t, 0:half1, :] = both[:, LANES * t:LANES * (t + 1)]

    @pl.loop(0, ROWS1 // 16, unroll=True)
    def _(i):
        z = zone(i, 1, 8)
        for c in range(CHAN):
            for t in range(2):
                add_up(v1, 2 * c + t, 16 * i, mask[z, t], w1[2 * c + t, tile(8 * i), :])

    sweep(s1, v1, w1, 0, tiles1, (1, 16), (0, 1), slabs1)
    sweep(s1, w1, v1, 0, tiles1, (1, 16), (0, 1), slabs1)

    for c in range(CHAN):
        both = move(v1[2 * c, 8:8 + rows1, :], double)
        for t in range(2):
            w0[3 * c + t, 8:8 + rows1, :] = both[:, LANES * t:LANES * (t + 1)]
        w0[3 * c + 2, 8:8 + rows1, :] = move(v1[2 * c + 1, 8:8 + rows1, :], double_sides)

    @pl.loop(0, tiles1, unroll=True)
    def _(i):
        z = zone(i, 1, 16)
        for c in range(CHAN):
            for t in range(3):
                add_up(v0, 3 * c + t, 8 + 16 * i, mask[z, t // 2], w0[3 * c + t, tile(8 + 8 * i), :])

    sweep(s0, v0, w0, 1, tiles0 - 2, (2, 32), (0, 0, 1), slabs0)

    act = mask[1, 0] * 0.2

    @pl.loop(0, BS // 8, unroll=True)
    def _(i):
        base = OWN0 + 8 * i
        for c in range(CHAN):
            centre, around = beside(w0, slabs0(c), base, lane, 2)
            for t in range(2):
                cols = slice(LANES * t, LANES * (t + 1))
                out[c, tile(8 * i), cols] = x_in[c, tile(8 * i), cols] + act * (
                    centre[t] + around[t] + s0[3 * c + t, tile(base), :])

    sent()
    sent_too()


def shards(groups, blks, image_a, image_b, initial, coverage, seam_label):
    vmem = lambda *dims: pltpu.VMEM(dims, F32)
    image = vmem(CHAN, BS, BS)
    scratch = [image] * 3
    scratch += [vmem(13, ROWS0, LANES), vmem(6, ROWS0, LANES)]
    scratch += [vmem(BS, LANES)] * 2 + [vmem(ROWS0, LANES)] * 2
    scratch += [vmem(3, 4, 8, LANES), vmem(3, 3, 8, LANES)]
    scratch += [vmem(9, ROWS0, LANES)] * 3 + [vmem(6, ROWS1, LANES)] * 3
    scratch += [vmem(3, ROWS2, LANES)] + [vmem(BS // 4, LANES)] * 2 + [vmem(ROWS2, LANES)] * 2
    scratch += [vmem(3, ROWS2, LANES)] * 3 + [vmem(3, ROWS3, LANES)] * 3
    scratch += [pltpu.SemaphoreType.DMA((4, 3))] + [pltpu.SemaphoreType.DMA((len(SENDS),))] * 4
    return pl.pallas_call(
        functools.partial(kernel, groups, blks),
        out_shape=pltpu.VMEM(image_a.shape, F32),
        in_specs=[pl.BlockSpec(memory_space=pl.ANY)] * 3 + [pl.BlockSpec(memory_space=pltpu.SMEM)] * 2,
        out_specs=pl.BlockSpec(memory_space=pltpu.VMEM),
        scratch_shapes=scratch,
        compiler_params=pltpu.CompilerParams(
            collective_id=0, has_side_effects=True, vmem_limit_bytes=40 << 20),
    )(*(pltpu.with_memory_space_constraint(i, pltpu.HBM) for i in (image_a, image_b, initial)), coverage, seam_label)


def solution(mesh):
    placed = (P(None, "group", "blk"),) * 3 + (P("group", "blk"),) * 2
    return jax.shard_map(
        functools.partial(shards, mesh.shape["group"], mesh.shape["blk"]),
        mesh=mesh, in_specs=placed, out_specs=P(None, "group", "blk"), check_vma=False)
```
